32 devices in a mesh: energy: 4 (over z), wire: 8 (over y, x, core).
Axes of the slice: x: 2, y: 2, z: 4, core: 2. Of those that a mesh axis runs over, the one named last changes fastest.
Arguments:
- g_prev: bfloat16 [2, 8, 8, 512, 512], P(None, 'energy', 'wire'), may hold values from -0.25 to 0.25
- local_green: bfloat16 [2, 8, 8, 512, 512], P(None, 'energy', 'wire'), may hold values from -0.09375 to 0.09375
- prop: bfloat16 [2, 8, 8, 512, 512], P(None, 'energy', 'wire'), may hold values from -1.5 to 1.5
- incoming: bfloat16 [2, 8, 8, 64, 512], P(None, 'energy', 'wire'), may hold values from -3 to 3
- plus_partner: int32 [8], replicated, may hold values from -1 to 7
- minus_partner: int32 [8], replicated, may hold values from -1 to 7
- counts: int32 [4], P('energy'), may hold values from 1 to 2
- pot_index: int32 [8], P('wire'), may hold values from 0 to 15
- levels: float32 [16], replicated, may hold values from -1 to 1
- coupling: float32 [2], replicated, may hold values from 0.5 to 2
Outputs:
- scattered: bfloat16 [2, 8, 8, 64, 512], P(None, 'energy', 'wire')
- green_next: bfloat16 [2, 8, 8, 512, 512], P(None, 'energy', 'wire')
The draws below stay inside these ranges and needn't reach their ends.
Inputs may be any that keep to these rules, and one draw needn't show every extreme that they name: `plus_partner`: -1 means that the partner energy lies outside the window. `minus_partner`: -1 means that the partner energy lies outside the window. The first counts[g] of the 2 slots of group g are live.
All inputs are finite; a program needn't handle non-finite values.
Results may differ from the reference program's by a relative error of at most 0.035.
Values may be sent and summed in bfloat16 or wider, within the bound.
No kernel may reach another device: no remote copies, remote signals or barrier semaphores. Data moves between devices by JAX's collectives and lax.ppermute only.
A program may use at most 192 MiB of HBM per device.

```python
import math
import jax
import jax.numpy as jnp
from jax import lax

BLOCK = 512
MODES = 64
ESLOT = 2
LEVELS = 16
GROUPS = 4
ENERGY_POINTS = 8
WIRE_SEGMENTS = 8


def draw_prop(key, part):
    split_keys = jax.random.split(key, 8)
    slow_share = 0.5
    slow_mask = jax.random.uniform(split_keys[0], (ENERGY_POINTS, BLOCK)) < slow_share
    slow_rate = math.log(10.0) / WIRE_SEGMENTS * jax.random.uniform(split_keys[1], (ENERGY_POINTS, BLOCK), minval=0.2, maxval=0.7)
    fast_rate = jax.random.uniform(split_keys[2], (ENERGY_POINTS, BLOCK), minval=0.4, maxval=1.2)
    damping_rate = jnp.where(slow_mask, slow_rate, fast_rate)
    broadening = jnp.exp(jax.random.uniform(split_keys[3], (ENERGY_POINTS, WIRE_SEGMENTS), minval=-0.7, maxval=0.7))
    sudden_event = jax.random.uniform(split_keys[4], (ENERGY_POINTS, WIRE_SEGMENTS)) < 3.0 / WIRE_SEGMENTS
    sudden_damping = jnp.where(sudden_event, jax.random.uniform(split_keys[5], (ENERGY_POINTS, WIRE_SEGMENTS), minval=0.5, maxval=0.8), 1.0)
    surviving_share = jnp.exp(-damping_rate[:, None, :] * broadening[:, :, None]) * sudden_damping[:, :, None]
    phase_angle = jax.random.uniform(split_keys[6], (ENERGY_POINTS, WIRE_SEGMENTS, BLOCK), minval=-math.pi, maxval=math.pi)
    scatter_noise = jax.random.normal(split_keys[7], (2, ENERGY_POINTS, WIRE_SEGMENTS, BLOCK, BLOCK)) * (0.25 / math.sqrt(2.0 * BLOCK))
    identity = (jnp.arange(BLOCK)[:, None] == jnp.arange(BLOCK)[None, :]).astype(jnp.float32)
    real_part = (identity * jnp.cos(phase_angle)[..., None, :] + scatter_noise[0]) * surviving_share[..., None, :]
    imag_part = (identity * jnp.sin(phase_angle)[..., None, :] + scatter_noise[1]) * surviving_share[..., None, :]
    return jnp.stack([real_part, imag_part]).astype(jnp.bfloat16)


def with_ends(result, stream_key, least, largest):
    dims = result.shape
    index_at = [jax.random.randint(jax.random.fold_in(stream_key, axis), (), 0, dims[axis]) for axis in range(len(dims))]
    result = result.at[tuple(index_at)].set(least)
    longest = dims.index(max(dims))
    index_at[longest] = (index_at[longest] + 1) % dims[longest]
    return result.at[tuple(index_at)].set(largest)


def block_levels(key, dims, shards, smallest, largest):
    def one(position, shards_of):
        steps = jax.random.uniform(jax.random.fold_in(jax.random.fold_in(key, 6), position), (shards_of,), jnp.float32, smallest / len(shards), largest / len(shards))
        return jnp.repeat(jnp.exp(steps), dims[position] // shards_of).reshape((-1,) + (1,) * (len(dims) - position - 1))

    gain = one(*shards[0])
    for cut in shards[1:]:
        gain = gain * one(*cut)
    return gain


def centred(own_key, dims, scale, limit, pieces=(), kind=jnp.bfloat16):
    level = block_levels(own_key, dims, pieces, -0.22, 0.18) if pieces else 1.0
    array = jax.random.normal(own_key, dims, jnp.float32) * scale * level
    return jnp.minimum(jnp.maximum(array, -limit), limit).astype(kind)


def setup_inputs(seed: int = 0) -> dict:
    splits = jax.random.split(jax.random.key(seed), 11)
    g_prev = centred(splits[0], (2, ENERGY_POINTS, WIRE_SEGMENTS, BLOCK, BLOCK), BLOCK ** -0.5, 0.25, ((1, 4), (2, 8)))
    local_green = centred(splits[1], (2, ENERGY_POINTS, WIRE_SEGMENTS, BLOCK, BLOCK), (BLOCK * WIRE_SEGMENTS) ** -0.5, 0.09375, ((1, 4), (2, 8)))
    prop = draw_prop(jax.random.fold_in(splits[10], 71), 0)
    incoming = centred(splits[3], (2, ENERGY_POINTS, WIRE_SEGMENTS, MODES, BLOCK), 0.5, 3.0, ((1, 4), (2, 8)))
    plus_partner = with_ends(jax.random.randint(splits[4], (ENERGY_POINTS,), -1, ENERGY_POINTS), jax.random.fold_in(splits[4], 1), -1, ENERGY_POINTS - 1).astype(jnp.int32)
    minus_partner = with_ends(jax.random.randint(splits[5], (ENERGY_POINTS,), -1, ENERGY_POINTS), jax.random.fold_in(splits[5], 1), -1, ENERGY_POINTS - 1).astype(jnp.int32)
    counts = with_ends(jax.random.randint(splits[6], (GROUPS,), 1, ESLOT + 1), jax.random.fold_in(splits[6], 1), 1, ESLOT).astype(jnp.int32)
    pot_index = with_ends(jax.random.randint(splits[7], (WIRE_SEGMENTS,), 0, LEVELS), jax.random.fold_in(splits[7], 1), 0, LEVELS - 1).astype(jnp.int32)
    levels = jnp.clip(jax.random.uniform(splits[8], (LEVELS,), jnp.float32, -1.0, 1.0), -1.0, 1.0)
    coupling = jnp.clip(jnp.exp(jax.random.uniform(splits[9], (2,), jnp.float32, math.log(0.5), math.log(2.0))), 0.5, 2.0)
    return dict(g_prev=g_prev, local_green=local_green, prop=prop, incoming=incoming, plus_partner=plus_partner, minus_partner=minus_partner, counts=counts, pot_index=pot_index, levels=levels, coupling=coupling)


def complex_product(first_op, second_op):
    first_op = first_op.astype(jnp.float32)
    second_op = second_op.astype(jnp.float32)

    def multiply(lhs_part, rhs_part):
        return jnp.einsum("...ij,...jk->...ik", lhs_part, rhs_part, precision=lax.Precision.HIGHEST)

    real_part = multiply(first_op[0], second_op[0]) - multiply(first_op[1], second_op[1])
    imag_part = multiply(first_op[0], second_op[1]) + multiply(first_op[1], second_op[0])
    return jnp.stack([real_part, imag_part])


def intersection(first_op, second_op):
    return jnp.einsum("smi,smj->sij", first_op, second_op, precision=lax.Precision.HIGHEST)


def reference(g_prev, local_green, prop, incoming, plus_partner, minus_partner, counts, pot_index, levels, coupling):
    level_hit = pot_index[:, None] == jnp.arange(LEVELS, dtype=jnp.int32)[None, :]
    potential = jnp.sum(jnp.where(level_hit, levels[None, :], jnp.float32(0.0)), axis=1)

    def one_energy(energy):
        plus_index = plus_partner[energy]
        minus_index = minus_partner[energy]
        upper_block = lax.dynamic_index_in_dim(g_prev, jnp.maximum(plus_index, 0).astype(jnp.int32), 1, False)
        lower_block = lax.dynamic_index_in_dim(g_prev, jnp.maximum(minus_index, 0).astype(jnp.int32), 1, False)
        upper_block = jnp.where(plus_index >= 0, upper_block, jnp.zeros_like(upper_block))
        lower_block = jnp.where(minus_index >= 0, lower_block, jnp.zeros_like(lower_block))
        incident = lax.dynamic_index_in_dim(incoming, energy, 1, False)
        shifted = coupling[0] * complex_product(incident, upper_block) + coupling[1] * complex_product(incident, lower_block)
        source_term = (shifted + potential[None, :, None, None] * incident.astype(jnp.float32)).astype(jnp.bfloat16)
        source = complex_product(source_term, lax.dynamic_index_in_dim(local_green, energy, 1, False))
        steps_here = lax.dynamic_index_in_dim(prop, energy, 1, False)

        def advance(amplitude, inputs):
            step_block, source_here = inputs
            advanced = (complex_product(amplitude, step_block) + source_here).astype(jnp.bfloat16)
            return advanced, advanced

        zero_wave = jnp.zeros((2, MODES, BLOCK), jnp.bfloat16)
        _, chained = lax.scan(advance, zero_wave, (jnp.moveaxis(steps_here, 1, 0), jnp.moveaxis(source, 1, 0)))
        chained = jnp.moveaxis(chained, 0, 1)
        combined = (incident.astype(jnp.float32) + chained.astype(jnp.float32)).astype(jnp.bfloat16)
        real_wave = combined[0].astype(jnp.float32)
        imag_wave = combined[1].astype(jnp.float32)
        green_real = (intersection(imag_wave, real_wave) - intersection(real_wave, imag_wave)) / MODES
        green_imag = (intersection(real_wave, real_wave) + intersection(imag_wave, imag_wave)) / MODES
        green_block = jnp.stack([green_real, green_imag])
        live_slot = (energy % ESLOT) < counts[energy // ESLOT]
        scattered_here = jnp.where(live_slot, chained, jnp.zeros_like(chained))
        green_here = jnp.where(live_slot, green_block, jnp.zeros_like(green_block)).astype(jnp.bfloat16)
        return scattered_here, green_here

    scattered, green_next = lax.map(one_energy, jnp.arange(ENERGY_POINTS, dtype=jnp.int32))
    return jnp.moveaxis(scattered, 0, 1), jnp.moveaxis(green_next, 0, 1)
```

```python
import functools

import jax
import jax.numpy as jnp
from jax import lax
from jax.experimental import pallas as pl
from jax.experimental.pallas import tpu as pltpu
from jax.sharding import PartitionSpec as P

VMEM = pl.BlockSpec(memory_space=pltpu.VMEM)
SMEM = pl.BlockSpec(memory_space=pltpu.SMEM)
F32, BF16 = jnp.float32, jnp.bfloat16


def params():
    return pltpu.CompilerParams(vmem_limit_bytes=40 << 20)


def dot(lhs, rhs):
    return jnp.dot(lhs, rhs, preferred_element_type=F32)


def times(lhs, rhs):
    return (
        dot(lhs[0], rhs[0]) - dot(lhs[1], rhs[1]),
        dot(lhs[0], rhs[1]) + dot(lhs[1], rhs[0]),
    )


def partner_kernel(shifts, groups, place, plus, minus, coupling, g_ref, *refs):
    count = len(shifts)
    waves, outs = refs[:count], refs[count:]
    group, core = place[0], place[1]
    slots = g_ref.shape[1]
    for n, shift in enumerate(shifts):
        owner = lax.rem(group + groups - shift, groups)
        for turn in range(slots):
            slot = core if turn == 0 else 1 - core
            target = owner * slots + slot
            wave = (waves[n][0, slot], waves[n][1, slot])
            real, imag = None, None
            for block in range(slots):
                name = group * slots + block
                weight = jnp.where(plus[target] == name, coupling[0], 0.0)
                weight += jnp.where(minus[target] == name, coupling[1], 0.0)
                part = times(wave, (g_ref[0, block], g_ref[1, block]))
                real = part[0] * weight if real is None else real + part[0] * weight
                imag = part[1] * weight if imag is None else imag + part[1] * weight
            out = outs[2 * n + turn]
            out[0] = real.astype(out.dtype)
            out[1] = imag.astype(out.dtype)


def partner_products(shifts, groups, place, plus, minus, coupling, g_here, waves):
    _, _, modes, orbitals = waves[0].shape
    return pl.pallas_call(
        functools.partial(partner_kernel, shifts, groups),
        out_shape=[jax.ShapeDtypeStruct((2, modes, orbitals), BF16)] * (2 * len(shifts)),
        in_specs=[SMEM] * 4 + [VMEM] * (1 + len(shifts)),
        out_specs=[VMEM] * (2 * len(shifts)),
        compiler_params=params(),
        name="partner_products",
    )(place, plus, minus, coupling, g_here, *waves)


def source_kernel(count, place, potential, incident, green, step, *refs):
    here, there = refs[:count], refs[count : 2 * count]
    first_ref, chip_ref, send_ref, term_ref = refs[2 * count :]
    core = place[1]
    for turn, parts in enumerate((here, there)):
        segment = core if turn == 0 else 1 - core
        for c in range(2):
            total = parts[0][c].astype(F32)
            for part in parts[1:]:
                total = total + part[c].astype(F32)
            total = total + potential[segment] * incident[segment, c].astype(F32)
            term_ref[segment, c] = total.astype(BF16)
    first = times((term_ref[0, 0], term_ref[0, 1]), (green[0, 0], green[0, 1]))
    first_ref[0], first_ref[1] = first
    rounded = (first[0].astype(BF16), first[1].astype(BF16))
    passed = times(rounded, (step[0], step[1]))
    added = times((term_ref[1, 0], term_ref[1, 1]), (green[1, 0], green[1, 1]))
    for c in range(2):
        chip = passed[c] + added[c]
        chip_ref[c] = chip
        send_ref[c] = chip.astype(BF16)


def chip_sources(place, potential, incident, green, step, here, there):
    _, _, modes, orbitals = incident.shape
    wave = (2, modes, orbitals)
    return pl.pallas_call(
        functools.partial(source_kernel, len(here)),
        out_shape=[
            jax.ShapeDtypeStruct(wave, F32),
            jax.ShapeDtypeStruct(wave, F32),
            jax.ShapeDtypeStruct(wave, BF16),
        ],
        in_specs=[SMEM] * 2 + [VMEM] * (3 + len(here) + len(there)),
        out_specs=[VMEM] * 3,
        scratch_shapes=[pltpu.VMEM((2, 2, modes, orbitals), BF16)],
        compiler_params=params(),
        name="chip_sources",
    )(place, potential, incident, green, step, *here, *there)


def chain_kernel(count, place, step, chip_map, first, chip, *refs):
    waves, maps = refs[:count], refs[count : 2 * count - 1]
    own_ref, other_ref, keep_ref = refs[2 * count - 1 :]
    core = place[1]
    entering = (waves[-1][0], waves[-1][1])
    for n in range(count - 2, -1, -1):
        moved = times(entering, (maps[n][0], maps[n][1]))
        entering = tuple((moved[c] + waves[n][c].astype(F32)).astype(BF16) for c in range(2))
    at_first = times(entering, (step[0], step[1]))
    at_second = times(entering, (chip_map[0], chip_map[1]))
    for c in range(2):
        keep_ref[0, c] = (at_first[c] + first[c]).astype(BF16)
        keep_ref[1, c] = (at_second[c] + chip[c]).astype(BF16)
    own_ref[...] = keep_ref[core]
    other_ref[...] = keep_ref[1 - core]


def chain(place, step, chip_map, first, chip, waves, maps):
    wave = first.shape
    return pl.pallas_call(
        functools.partial(chain_kernel, len(waves)),
        out_shape=[jax.ShapeDtypeStruct(wave, BF16)] * 2,
        in_specs=[SMEM] + [VMEM] * (4 + len(waves) + len(maps)),
        out_specs=[VMEM] * 2,
        scratch_shapes=[pltpu.VMEM((2,) + wave, BF16)],
        compiler_params=params(),
        name="chain",
    )(place, step, chip_map, first, chip, *waves, *maps)


def across(lhs, rhs):
    return lax.dot_general(lhs, rhs, (((0,), (0,)), ((), ())), preferred_element_type=F32)


def block_kernel(place, counts, incident, own, other, scattered, green_next, both):
    core = place[1]
    modes = own.shape[1]
    for turn, chained in enumerate((own, other)):
        slot = core if turn == 0 else 1 - core
        live = slot < counts[0]
        for c in range(2):
            wave = chained[c].astype(F32)
            scattered[c, slot] = jnp.where(live, wave, 0.0).astype(BF16)
            combined = (incident[c, slot].astype(F32) + wave).astype(BF16)
            both[0, c * modes : (c + 1) * modes] = combined
            both[1, (1 - c) * modes : (2 - c) * modes] = -combined if c == 0 else combined
        stacked = both[0]
        real = across(both[1], stacked) / modes
        imag = across(stacked, stacked) / modes
        green_next[0, slot] = jnp.where(live, real, 0.0).astype(BF16)
        green_next[1, slot] = jnp.where(live, imag, 0.0).astype(BF16)


def green_blocks(place, counts, incident, own, other):
    _, slots, modes, orbitals = incident.shape
    return pl.pallas_call(
        block_kernel,
        out_shape=[
            jax.ShapeDtypeStruct((2, slots, modes, orbitals), BF16),
            jax.ShapeDtypeStruct((2, slots, orbitals, orbitals), BF16),
        ],
        in_specs=[SMEM] * 2 + [VMEM] * 3,
        out_specs=[VMEM] * 2,
        scratch_shapes=[pltpu.VMEM((2, 2 * modes, orbitals), BF16)],
        compiler_params=params(),
        name="green_blocks",
    )(place, counts, incident, own, other)


def complex_matrix(lhs, rhs):
    real = dot(lhs[0], rhs[0]) - dot(lhs[1], rhs[1])
    imag = dot(lhs[0], rhs[1]) + dot(lhs[1], rhs[0])
    return jnp.stack([real, imag])


def shards(groups, segments, g_prev, local_green, prop, incoming, plus_partner, minus_partner, counts, pot_index, levels, coupling):
    chips = segments // 2
    group, segment = lax.axis_index("energy"), lax.axis_index("wire")
    core = lax.rem(segment, 2)
    place = jnp.stack([group, core]).astype(jnp.int32)
    g_here, green_here = g_prev[:, :, 0], local_green[:, :, 0]
    prop_here, incident = prop[:, :, 0], incoming[:, :, 0]

    def turned(shift, swap):
        pairs = []
        for e in range(groups):
            for w in range(segments):
                pairs.append((e * segments + w, (e + shift) % groups * segments + (w ^ swap)))
        return pairs

    def send(value, shift, swap):
        return lax.ppermute(value, ("energy", "wire"), turned(shift, swap))

    def later(value, hops, least=0):
        pairs = []
        for chip in range(least, chips - hops):
            pairs += [(2 * chip + b, 2 * (chip + hops) + b) for b in range(2)]
        return lax.ppermute(value, "wire", pairs)

    waves = [incident] + [send(incident, shift, 0) for shift in range(1, groups)]

    def by_segment(value, axis):
        mine = lax.dynamic_index_in_dim(value, core, axis, False)
        passed = lax.dynamic_index_in_dim(value, 1 - core, axis, False)
        received = send(passed, 0, 1)
        first = jnp.where(core == 0, mine, received)
        second = jnp.where(core == 0, received, mine)
        return first, second

    level_hit = pot_index[0] == jnp.arange(levels.shape[0], dtype=jnp.int32)
    potential = jnp.sum(jnp.where(level_hit, levels, F32(0.0)))[None]
    potential_there = send(potential, 0, 1)
    potentials = jnp.where(
        core == 0,
        jnp.concatenate([potential, potential_there]),
        jnp.concatenate([potential_there, potential]),
    )
    steps = by_segment(prop_here, 1)
    chip_map = complex_matrix(*steps).astype(BF16)
    greens = jnp.stack(by_segment(green_here, 1))
    incidents = jnp.stack(by_segment(incident, 1))

    shifts = tuple(range(groups))
    local = partner_products((0,), groups, place, plus_partner, minus_partner, coupling, g_here, waves[:1])
    far = partner_products(shifts[1:], groups, place, plus_partner, minus_partner, coupling, g_here, waves[1:])
    here, there = [local[0]], [send(local[1], 0, 1)]
    for n, shift in enumerate(shifts[1:]):
        here.append(send(far[2 * n], groups - shift, 0))
        there.append(send(far[2 * n + 1], groups - shift, 1))

    first, chip, chip_send = chip_sources(place, potentials, incidents, greens, steps[1], here, there)
    if chips <= 4:
        maps = [later(chip_map, hops, 1) for hops in range(1, chips - 1)]
        arrived = [later(chip_send, hops) for hops in range(1, chips)]
    else:
        maps = []
        entering = jnp.zeros_like(chip_send)
        for at in range(chips - 1):
            leaving = (complex_matrix(entering, chip_map) + chip).astype(BF16)
            pairs = [(2 * at + b, 2 * at + 2 + b) for b in range(2)]
            entering = entering + lax.ppermute(leaving, "wire", pairs)
        arrived = [entering]
    own, other = chain(place, steps[0], chip_map, first, chip, arrived, maps)

    other = send(other, 0, 1)
    scattered, green_next = green_blocks(place, counts, incident, own, other)
    return scattered[:, :, None], green_next[:, :, None]


def solution(mesh):
    placed = P(None, "energy", "wire", None, None)
    return jax.shard_map(
        functools.partial(shards, mesh.shape["energy"], mesh.shape["wire"]),
        mesh=mesh,
        in_specs=(placed,) * 4 + (P(), P(), P("energy"), P("wire"), P(), P()),
        out_specs=(placed, placed),
        check_vma=False,
    )
```

```python
import functools

import jax
import jax.numpy as jnp
from jax import lax
from jax.experimental import pallas as pl
from jax.experimental.pallas import tpu as pltpu
from jax.sharding import PartitionSpec as P

VMEM = pl.BlockSpec(memory_space=pltpu.VMEM)
SMEM = pl.BlockSpec(memory_space=pltpu.SMEM)
COST = 1000000000
F32, BF16 = jnp.float32, jnp.bfloat16


def call(kernel, name, outs, scalars, arrays, scratch=()):
    shapes = [jax.ShapeDtypeStruct(shape, kind) for shape, kind in outs]
    moved = sum(x.size * x.dtype.itemsize for x in list(arrays) + shapes)
    return pl.pallas_call(
        kernel,
        out_shape=shapes,
        in_specs=[SMEM] * len(scalars) + [VMEM] * len(arrays),
        out_specs=[VMEM] * len(outs),
        scratch_shapes=[pltpu.VMEM(shape, kind) for shape, kind in scratch],
        compiler_params=pltpu.CompilerParams(vmem_limit_bytes=16 << 20),
        cost_estimate=pl.CostEstimate(flops=COST, bytes_accessed=1, transcendentals=0),
        name=name,
    )(*scalars, *arrays)


def this_core():
    return lax.rem(lax.axis_index("wire"), 2)


def dot(lhs, rhs):
    return jnp.dot(lhs, rhs, preferred_element_type=F32)


def times(lhs, rhs):
    return (
        dot(lhs[0], rhs[0]) - dot(lhs[1], rhs[1]),
        dot(lhs[0], rhs[1]) + dot(lhs[1], rhs[0]),
    )


def pair(ref, *index):
    return ref[(0,) + index], ref[(1,) + index]


def weighted(slot, owner, whole, real_valued, wave_ref, g_ref, total):
    slots = g_ref.shape[1]
    energies = whole.shape[0] // 2
    group, target = lax.axis_index("energy"), owner * slots + slot
    total[...] = jnp.zeros_like(total)
    for block in range(slots):
        name = group * slots + block
        weight = jnp.where(whole[target] == name, real_valued[0], 0.0)
        weight += jnp.where(whole[energies + target] == name, real_valued[1], 0.0)

        @pl.when(weight != 0.0)
        def _():
            real, imag = times(pair(wave_ref, slot), pair(g_ref, block))
            total[0] += real * weight
            total[1] += imag * weight


def product_kernel(offset, whole, real_valued, wave_ref, g_ref, out_ref, total):
    group = lax.axis_index("energy")
    for slot in range(g_ref.shape[1]):
        weighted(slot, group ^ offset, whole, real_valued, wave_ref, g_ref, total)
        for c in range(2):
            out_ref[c, slot] = total[c].astype(BF16)


def own_kernel(whole, real_valued, wave_ref, g_ref, out_ref, total):
    group = lax.axis_index("energy")
    potential = real_valued[2 + whole[whole.shape[0] - 1]]
    for slot in range(g_ref.shape[1]):
        weighted(slot, group, whole, real_valued, wave_ref, g_ref, total)
        for c in range(2):
            out_ref[c, slot] = total[c] + potential * wave_ref[c, slot].astype(F32)


def term_kernel(base, *refs):
    parts, outs = refs[:-2], refs[-2:]
    core = this_core()
    for out_ref, slot in zip(outs, (core, 1 - core)):
        for c in range(2):
            total = base[c, slot]
            for part in parts:
                total = total + part[c, slot].astype(F32)
            out_ref[c] = total.astype(BF16)


def prepare_kernel(prop, prop_other, green, green_other, steps, greens, chip_map, arrived):
    core = this_core()
    copies = []
    for n, (source, target) in enumerate(((prop, steps), (prop_other, steps), (green, greens), (green_other, greens))):
        segment = core if n % 2 == 0 else 1 - core
        copies += [
            pltpu.make_async_copy(source.at[c, core], target.at[segment, c], arrived.at[n, c])
            for c in range(2)
        ]
    for copy in copies:
        copy.start()
    for copy in copies[:4]:
        copy.wait()
    second = (steps[1, 0], steps[1, 1])
    half = steps.shape[2] // 2
    for rows in (slice(0, half), slice(half, None)):
        moved = times((steps[0, 0, rows], steps[0, 1, rows]), second)
        for c in range(2):
            chip_map[c, rows] = moved[c].astype(BF16)
    for copy in copies[4:]:
        copy.wait()


def source_kernel(own, other, steps, greens, first_ref, chip_ref, send_ref, term):
    core = this_core()
    term[core], term[1 - core] = own[...], other[...]
    first = times((term[0, 0], term[0, 1]), (greens[0, 0], greens[0, 1]))
    first_ref[0], first_ref[1] = first
    rounded = (first[0].astype(BF16), first[1].astype(BF16))
    passed = times(rounded, (steps[1, 0], steps[1, 1]))
    added = times((term[1, 0], term[1, 1]), (greens[1, 0], greens[1, 1]))
    for c in range(2):
        chip = passed[c] + added[c]
        chip_ref[c] = chip
        send_ref[c] = chip.astype(BF16)


def chain_kernel(count, steps, chip_map, first, chip, *refs):
    waves, maps = refs[:count], refs[count : 2 * count - 1]
    own_ref, other_ref, keep = refs[2 * count - 1 :]
    core = this_core()
    entering = (waves[-1][0], waves[-1][1])
    for n in range(count - 2, -1, -1):
        moved = times(entering, (maps[n][0], maps[n][1]))
        entering = tuple((moved[c] + waves[n][c].astype(F32)).astype(BF16) for c in range(2))
    at_first = times(entering, (steps[0, 0], steps[0, 1]))
    at_second = times(entering, (chip_map[0], chip_map[1]))
    for c in range(2):
        keep[0, c] = (at_first[c] + first[c]).astype(BF16)
        keep[1, c] = (at_second[c] + chip[c]).astype(BF16)
    own_ref[...] = keep[core]
    other_ref[...] = keep[1 - core]


def across(lhs, rhs):
    return lax.dot_general(lhs, rhs, (((0,), (0,)), ((), ())), preferred_element_type=F32)


def block_kernel(counts, incident, own, other, scattered, green_next, both):
    core = this_core()
    modes = own.shape[1]
    for turn, chained in enumerate((own, other)):
        slot = core if turn == 0 else 1 - core
        live = slot < counts[0]
        for c in range(2):
            wave = chained[c].astype(F32)
            scattered[c, slot] = jnp.where(live, wave, 0.0).astype(BF16)
            combined = (incident[c, slot].astype(F32) + wave).astype(BF16)
            both[0, c * modes : (c + 1) * modes] = combined
            both[1, (1 - c) * modes : (2 - c) * modes] = -combined if c == 0 else combined
        stacked = both[0]
        real = across(both[1], stacked) / modes
        imag = across(stacked, stacked) / modes
        green_next[0, slot] = jnp.where(live, real, 0.0).astype(BF16)
        green_next[1, slot] = jnp.where(live, imag, 0.0).astype(BF16)


def complex_matrix(lhs, rhs):
    return jnp.stack(times(lhs, rhs))


def shards(groups, segments, g_prev, local_green, prop, incoming, plus_partner, minus_partner, counts, pot_index, levels, coupling):
    chips = segments // 2
    g_here, green_here = g_prev[:, :, 0], local_green[:, :, 0]
    prop_here, incident = prop[:, :, 0], incoming[:, :, 0]
    _, slots, modes, orbitals = incident.shape
    wave, block = (2, modes, orbitals), (2, orbitals, orbitals)

    def hbm(value):
        return pltpu.with_memory_space_constraint(value, pltpu.MemorySpace.HBM)

    def swap(value, offset, turn=0):
        pairs = [
            (e * segments + w, (e ^ offset) * segments + (w ^ turn))
            for e in range(groups)
            for w in range(segments)
        ]
        return lax.ppermute(value, ("energy", "wire"), pairs)

    def later(value, hops, least=0):
        pairs = []
        for chip in range(least, chips - hops):
            pairs += [(2 * chip + b, 2 * (chip + hops) + b) for b in range(2)]
        return lax.ppermute(value, "wire", pairs)

    scalars = [
        jnp.concatenate([plus_partner, minus_partner, pot_index]),
        jnp.concatenate([coupling, levels]),
    ]
    total = [(wave, F32)]
    every = (2, slots, modes, orbitals)

    waves = [incident] + [None] * (groups - 1)
    if True:
        for offset in range(1, groups):
            if offset == 1 or offset % 2 == 0:
                waves[offset] = swap(incident, offset)
        prop_other, green_other = swap(prop_here, 0, 1), swap(green_here, 0, 1)
        base = call(own_kernel, "own", [(every, F32)], scalars, [incident, g_here], total)[0]
        steps, greens, chip_map = pl.pallas_call(
            prepare_kernel,
            out_shape=[
                jax.ShapeDtypeStruct((2,) + block, BF16),
                jax.ShapeDtypeStruct((2,) + block, BF16),
                jax.ShapeDtypeStruct(block, BF16),
            ],
            in_specs=[pl.BlockSpec(memory_space=pltpu.MemorySpace.HBM), pl.BlockSpec(memory_space=pl.ANY)] * 2,
            out_specs=[VMEM] * 3,
            scratch_shapes=[pltpu.SemaphoreType.DMA((4, 2))],
            compiler_params=pltpu.CompilerParams(vmem_limit_bytes=16 << 20),
            cost_estimate=pl.CostEstimate(flops=COST, bytes_accessed=1, transcendentals=0),
            name="prepare",
        )(hbm(prop_here), prop_other, hbm(green_here), green_other)
    waves[1], waves[2], chip_map, base = lax.optimization_barrier((waves[1], waves[2], chip_map, base))
    for offset in range(3, groups, 2):
        waves[offset] = swap(waves[offset - 1], 1)

    back = []
    for offset in range(1, groups):
        part = call(
            functools.partial(product_kernel, offset), "product", [(every, BF16)], scalars, [waves[offset], g_here], total
        )[0]
        if offset == 1:
            part, waves[-1] = lax.optimization_barrier((part, waves[-1]))
        if offset == 2:
            part, chip_map = lax.optimization_barrier((part, chip_map))
        back.append(swap(part, offset))
    own, other = call(term_kernel, "term", [(wave, BF16)] * 2, [], [base] + back)
    other = swap(other, 0, 1)

    first, chip, chip_send = call(
        source_kernel,
        "source",
        [(wave, F32), (wave, F32), (wave, BF16)],
        [],
        [own, other, steps, greens],
        [((2,) + wave, BF16)])
    if chips <= 4:
        maps = [later(chip_map, hops, 1) for hops in range(1, chips - 1)]
        arrived = [later(chip_send, hops) for hops in range(1, chips)]
    else:
        maps = []
        entering = jnp.zeros_like(chip_send)
        for at in range(chips - 1):
            leaving = (complex_matrix(entering, chip_map) + chip).astype(BF16)
            pairs = [(2 * at + b, 2 * at + 2 + b) for b in range(2)]
            entering = entering + lax.ppermute(leaving, "wire", pairs)
        arrived = [entering]
    own, other = call(
        functools.partial(chain_kernel, len(arrived)),
        "chain",
        [(wave, BF16)] * 2,
        [],
        [steps, chip_map, first, chip] + arrived + maps,
        [((2,) + wave, BF16)])

    other = swap(other, 0, 1)
    scattered, green_next = call(
        block_kernel,
        "green_blocks",
        [((2, slots, modes, orbitals), BF16), ((2, slots, orbitals, orbitals), BF16)],
        [counts],
        [incident, own, other],
        [((2, 2 * modes, orbitals), BF16)])
    return scattered[:, :, None], green_next[:, :, None]


def solution(mesh):
    placed = P(None, "energy", "wire", None, None)
    return jax.shard_map(
        functools.partial(shards, mesh.shape["energy"], mesh.shape["wire"]),
        mesh=mesh,
        in_specs=(placed,) * 4 + (P(), P(), P("energy"), P("wire"), P(), P()),
        out_specs=(placed, placed),
        check_vma=False,
    )
```

```python
import functools

import jax
import jax.numpy as jnp
from jax import lax
from jax.experimental import pallas as pl
from jax.experimental.pallas import tpu as pltpu
from jax.sharding import PartitionSpec as P

VMEM = pl.BlockSpec(memory_space=pltpu.VMEM)
SMEM = pl.BlockSpec(memory_space=pltpu.SMEM)
COST = 3000000000
F32, BF16 = jnp.float32, jnp.bfloat16


def call(kernel, name, outs, scalars, arrays, scratch=()):
    shapes = [jax.ShapeDtypeStruct(shape, kind) for shape, kind in outs]
    moved = sum(x.size * x.dtype.itemsize for x in list(arrays) + shapes)
    return pl.pallas_call(
        kernel,
        out_shape=shapes,
        in_specs=[SMEM] * len(scalars) + [VMEM] * len(arrays),
        out_specs=[VMEM] * len(outs),
        scratch_shapes=[pltpu.VMEM(shape, kind) for shape, kind in scratch],
        compiler_params=pltpu.CompilerParams(vmem_limit_bytes=16 << 20),
        cost_estimate=pl.CostEstimate(flops=COST, bytes_accessed=1, transcendentals=0),
        name=name,
    )(*scalars, *arrays)


def this_core():
    return lax.rem(lax.axis_index("wire"), 2)


def dot(lhs, rhs):
    return jnp.dot(lhs, rhs, preferred_element_type=F32)


def times(lhs, rhs):
    rows = lhs[0].shape[0]
    both = jnp.concatenate([lhs[0], lhs[1]], axis=0)
    by_real, by_imag = dot(both, rhs[0]), dot(both, rhs[1])
    return by_real[:rows] - by_imag[rows:], by_imag[:rows] + by_real[rows:]


def pair(ref, *index):
    return ref[(0,) + index], ref[(1,) + index]


def weighted(slot, owner, whole, real_valued, wave_ref, g_ref, total):
    slots = g_ref.shape[1]
    energies = whole.shape[0] // 2
    group, target = lax.axis_index("energy"), owner * slots + slot
    total[...] = jnp.zeros_like(total)
    for block in range(slots):
        name = group * slots + block
        weight = jnp.where(whole[target] == name, real_valued[0], 0.0)
        weight += jnp.where(whole[energies + target] == name, real_valued[1], 0.0)

        @pl.when(weight != 0.0)
        def _():
            real, imag = times(pair(wave_ref, slot), pair(g_ref, block))
            total[0] += real * weight
            total[1] += imag * weight


def product_kernel(offset, whole, real_valued, wave_ref, g_ref, out_ref, total):
    group = lax.axis_index("energy")
    for slot in range(g_ref.shape[1]):
        weighted(slot, group ^ offset, whole, real_valued, wave_ref, g_ref, total)
        for c in range(2):
            out_ref[c, slot] = total[c].astype(BF16)


def own_kernel(whole, real_valued, wave_ref, g_ref, out_ref, total):
    group = lax.axis_index("energy")
    potential = real_valued[2 + whole[whole.shape[0] - 1]]
    for slot in range(g_ref.shape[1]):
        weighted(slot, group, whole, real_valued, wave_ref, g_ref, total)
        for c in range(2):
            out_ref[c, slot] = total[c] + potential * wave_ref[c, slot].astype(F32)


def term_kernel(base, *refs):
    parts, outs = refs[:-2], refs[-2:]
    core = this_core()
    for out_ref, slot in zip(outs, (core, 1 - core)):
        for c in range(2):
            total = base[c, slot]
            for part in parts:
                total = total + part[c, slot].astype(F32)
            out_ref[c] = total.astype(BF16)


def prepare_kernel(prop, prop_other, green, green_other, steps, greens, chip_map, arrived):
    core = this_core()
    copies = []
    for n, (source, target) in enumerate(((prop, steps), (prop_other, steps), (green, greens), (green_other, greens))):
        segment = core if n % 2 == 0 else 1 - core
        copies += [
            pltpu.make_async_copy(source.at[c, core], target.at[segment, c], arrived.at[n, c])
            for c in range(2)
        ]
    for copy in copies:
        copy.start()
    for copy in copies[:4]:
        copy.wait()
    second = (steps[1, 0], steps[1, 1])
    half = steps.shape[2] // 2
    for rows in (slice(0, half), slice(half, None)):
        moved = times((steps[0, 0, rows], steps[0, 1, rows]), second)
        for c in range(2):
            chip_map[c, rows] = moved[c].astype(BF16)
    for copy in copies[4:]:
        copy.wait()


def source_kernel(own, other, steps, greens, first_ref, chip_ref, send_ref, term):
    core = this_core()
    term[core], term[1 - core] = own[...], other[...]
    first = times((term[0, 0], term[0, 1]), (greens[0, 0], greens[0, 1]))
    first_ref[0], first_ref[1] = first
    rounded = (first[0].astype(BF16), first[1].astype(BF16))
    passed = times(rounded, (steps[1, 0], steps[1, 1]))
    added = times((term[1, 0], term[1, 1]), (greens[1, 0], greens[1, 1]))
    for c in range(2):
        chip = passed[c] + added[c]
        chip_ref[c] = chip
        send_ref[c] = chip.astype(BF16)


def chain_kernel(count, steps, chip_map, first, chip, *refs):
    waves, maps = refs[:count], refs[count : 2 * count - 1]
    own_ref, other_ref, keep = refs[2 * count - 1 :]
    core = this_core()
    entering = (waves[-1][0], waves[-1][1])
    for n in range(count - 2, -1, -1):
        moved = times(entering, (maps[n][0], maps[n][1]))
        entering = tuple((moved[c] + waves[n][c].astype(F32)).astype(BF16) for c in range(2))
    at_first = times(entering, (steps[0, 0], steps[0, 1]))
    at_second = times(entering, (chip_map[0], chip_map[1]))
    for c in range(2):
        keep[0, c] = (at_first[c] + first[c]).astype(BF16)
        keep[1, c] = (at_second[c] + chip[c]).astype(BF16)
    own_ref[...] = keep[core]
    other_ref[...] = keep[1 - core]


def across(lhs, rhs):
    return lax.dot_general(lhs, rhs, (((0,), (0,)), ((), ())), preferred_element_type=F32)


def block_kernel(turn, counts, incident, chained, *refs):
    scattered, green_next, both, waves, blocks, sent = refs[-6:]
    core = this_core()
    slot = core if turn == 0 else 1 - core
    live = slot < counts[0]
    modes = chained.shape[1]
    copies = []
    for c in range(2):
        wave = chained[c].astype(F32)
        waves[c] = jnp.where(live, wave, 0.0).astype(BF16)
        copies.append(pltpu.make_async_copy(waves.at[c], scattered.at[c, slot], sent.at[c]))
        copies[-1].start()
        combined = (incident[c, slot].astype(F32) + wave).astype(BF16)
        both[0, c * modes : (c + 1) * modes] = combined
        both[1, (1 - c) * modes : (2 - c) * modes] = -combined if c == 0 else combined
    stacked = both[0]
    for c in range(2):
        block = across(both[1 - c], stacked) / modes
        blocks[c] = jnp.where(live, block, 0.0).astype(BF16)
        copies.append(pltpu.make_async_copy(blocks.at[c], green_next.at[c, slot], sent.at[2 + c]))
        copies[-1].start()
    for copy in copies:
        copy.wait()


def green_blocks(turn, counts, incident, chained, filled=()):
    _, slots, modes, orbitals = incident.shape
    anywhere = pl.BlockSpec(memory_space=pl.ANY)
    return pl.pallas_call(
        functools.partial(block_kernel, turn),
        out_shape=[
            jax.ShapeDtypeStruct((2, slots, modes, orbitals), BF16),
            jax.ShapeDtypeStruct((2, slots, orbitals, orbitals), BF16),
        ],
        in_specs=[SMEM, VMEM, VMEM] + [anywhere] * len(filled),
        out_specs=[anywhere] * 2,
        input_output_aliases={3 + n: n for n in range(len(filled))},
        scratch_shapes=[
            pltpu.VMEM((2, 2 * modes, orbitals), BF16),
            pltpu.VMEM((2, modes, orbitals), BF16),
            pltpu.VMEM((2, orbitals, orbitals), BF16),
            pltpu.SemaphoreType.DMA((4,)),
        ],
        compiler_params=pltpu.CompilerParams(vmem_limit_bytes=16 << 20),
        cost_estimate=pl.CostEstimate(flops=COST, bytes_accessed=1, transcendentals=0),
        name="green_blocks",
    )(counts, incident, chained, *filled)


def complex_matrix(lhs, rhs):
    return jnp.stack(times(lhs, rhs))


def shards(groups, segments, g_prev, local_green, prop, incoming, plus_partner, minus_partner, counts, pot_index, levels, coupling):
    chips = segments // 2
    g_here, green_here = g_prev[:, :, 0], local_green[:, :, 0]
    prop_here, incident = prop[:, :, 0], incoming[:, :, 0]
    _, slots, modes, orbitals = incident.shape
    wave, block = (2, modes, orbitals), (2, orbitals, orbitals)

    def hbm(value):
        return pltpu.with_memory_space_constraint(value, pltpu.MemorySpace.HBM)

    def swap(value, offset, turn=0):
        pairs = [
            (e * segments + w, (e ^ offset) * segments + (w ^ turn))
            for e in range(groups)
            for w in range(segments)
        ]
        return lax.ppermute(value, ("energy", "wire"), pairs)

    def later(value, hops, least=0):
        pairs = []
        for chip in range(least, chips - hops):
            pairs += [(2 * chip + b, 2 * (chip + hops) + b) for b in range(2)]
        return lax.ppermute(value, "wire", pairs)

    scalars = [
        jnp.concatenate([plus_partner, minus_partner, pot_index]),
        jnp.concatenate([coupling, levels]),
    ]
    total = [(wave, F32)]
    every = (2, slots, modes, orbitals)

    waves = [incident] + [None] * (groups - 1)
    for _ in range(1):
        for offset in range(groups - 1, 0, -1):
            if offset == 1 or offset % 2 == 0:
                waves[offset] = swap(incident, offset)
        prop_other, green_other = swap(prop_here, 0, 1), swap(green_here, 0, 1)
        steps, greens, chip_map = pl.pallas_call(
            prepare_kernel,
            out_shape=[
                jax.ShapeDtypeStruct((2,) + block, BF16),
                jax.ShapeDtypeStruct((2,) + block, BF16),
                jax.ShapeDtypeStruct(block, BF16),
            ],
            in_specs=[pl.BlockSpec(memory_space=pltpu.MemorySpace.HBM), pl.BlockSpec(memory_space=pl.ANY)] * 2,
            out_specs=[VMEM] * 3,
            scratch_shapes=[pltpu.SemaphoreType.DMA((4, 2))],
            compiler_params=pltpu.CompilerParams(vmem_limit_bytes=16 << 20),
            cost_estimate=pl.CostEstimate(flops=COST, bytes_accessed=1, transcendentals=0),
            name="prepare",
        )(hbm(prop_here), prop_other, hbm(green_here), green_other)
    waves[1], waves[2], _ = lax.optimization_barrier((waves[1], waves[2], chip_map))
    for offset in range(3, groups, 2):
        waves[offset] = swap(waves[offset - 1], 1)

    parts = [
        call(
            functools.partial(product_kernel, offset), "product", [(every, BF16)], scalars, [waves[offset], g_here], total
        )[0]
        for offset in range(1, groups)
    ]
    parts[0], parts[-1] = lax.optimization_barrier((parts[0], parts[-1]))
    back = [swap(part, offset + 1) for offset, part in enumerate(parts)]
    waves[0], parts[-1] = lax.optimization_barrier((incident, parts[-1]))
    base = call(own_kernel, "own", [(every, F32)], scalars, [waves[0], g_here], total)[0]
    own, other = call(term_kernel, "term", [(wave, BF16)] * 2, [], [base] + back)
    other = swap(other, 0, 1)

    first, chip, chip_send = call(
        source_kernel,
        "source",
        [(wave, F32), (wave, F32), (wave, BF16)],
        [],
        [own, other, steps, greens],
        [((2,) + wave, BF16)])
    if chips <= 4:
        maps = [later(chip_map, hops, 1) for hops in range(1, chips - 1)]
        arrived = [later(chip_send, hops) for hops in range(1, chips)]
    else:
        maps = []
        entering = jnp.zeros_like(chip_send)
        for at in range(chips - 1):
            leaving = (complex_matrix(entering, chip_map) + chip).astype(BF16)
            pairs = [(2 * at + b, 2 * at + 2 + b) for b in range(2)]
            entering = entering + lax.ppermute(leaving, "wire", pairs)
        arrived = [entering]
    own, other = call(
        functools.partial(chain_kernel, len(arrived)),
        "chain",
        [(wave, BF16)] * 2,
        [],
        [steps, chip_map, first, chip] + arrived + maps,
        [((2,) + wave, BF16)])

    other = swap(other, 0, 1)
    filled = green_blocks(0, counts, incident, own)
    scattered, green_next = green_blocks(1, counts, incident, other, filled)
    return scattered[:, :, None], green_next[:, :, None]


def solution(mesh):
    placed = P(None, "energy", "wire", None, None)
    return jax.shard_map(
        functools.partial(shards, mesh.shape["energy"], mesh.shape["wire"]),
        mesh=mesh,
        in_specs=(placed,) * 4 + (P(), P(), P("energy"), P("wire"), P(), P()),
        out_specs=(placed, placed),
        check_vma=False,
    )
```

```python
import functools

import jax
import jax.numpy as jnp
from jax import lax
from jax.experimental import pallas as pl
from jax.experimental.pallas import tpu as pltpu
from jax.sharding import PartitionSpec as P

VMEM = pl.BlockSpec(memory_space=pltpu.VMEM)
SMEM = pl.BlockSpec(memory_space=pltpu.SMEM)
COST = 3000000000
F32, BF16 = jnp.float32, jnp.bfloat16


def call(kernel, name, outs, scalars, arrays, scratch=()):
    shapes = [jax.ShapeDtypeStruct(shape, kind) for shape, kind in outs]
    moved = sum(x.size * x.dtype.itemsize for x in list(arrays) + shapes)
    return pl.pallas_call(
        kernel,
        out_shape=shapes,
        in_specs=[SMEM] * len(scalars) + [VMEM] * len(arrays),
        out_specs=[VMEM] * len(outs),
        scratch_shapes=[pltpu.VMEM(shape, kind) for shape, kind in scratch],
        compiler_params=pltpu.CompilerParams(vmem_limit_bytes=16 << 20),
        cost_estimate=pl.CostEstimate(flops=COST, bytes_accessed=1, transcendentals=0),
        name=name,
    )(*scalars, *arrays)


def this_core():
    return lax.rem(lax.axis_index("wire"), 2)


def dot(lhs, rhs):
    return jnp.dot(lhs, rhs, preferred_element_type=F32)


def times(lhs, rhs):
    rows = lhs[0].shape[0]
    both = jnp.concatenate([lhs[0], lhs[1]], axis=0)
    by_real, by_imag = dot(both, rhs[0]), dot(both, rhs[1])
    return by_real[:rows] - by_imag[rows:], by_imag[:rows] + by_real[rows:]


def pair(ref, *index):
    return ref[(0,) + index], ref[(1,) + index]


def weighted(slot, owner, whole, real_valued, wave_ref, g_ref, total):
    slots = g_ref.shape[1]
    energies = whole.shape[0] // 2
    group, target = lax.axis_index("energy"), owner * slots + slot
    total[...] = jnp.zeros_like(total)
    for block in range(slots):
        name = group * slots + block
        weight = jnp.where(whole[target] == name, real_valued[0], 0.0)
        weight += jnp.where(whole[energies + target] == name, real_valued[1], 0.0)

        @pl.when(weight != 0.0)
        def _():
            real, imag = times(pair(wave_ref, slot), pair(g_ref, block))
            total[0] += real * weight
            total[1] += imag * weight


def product_kernel(offset, whole, real_valued, wave_ref, g_ref, out_ref, total):
    group = lax.axis_index("energy")
    for slot in range(g_ref.shape[1]):
        weighted(slot, group ^ offset, whole, real_valued, wave_ref, g_ref, total)
        for c in range(2):
            out_ref[c, slot] = total[c].astype(BF16)


def own_kernel(whole, real_valued, wave_ref, g_ref, out_ref, total):
    group = lax.axis_index("energy")
    potential = real_valued[2 + whole[whole.shape[0] - 1]]
    for slot in range(g_ref.shape[1]):
        weighted(slot, group, whole, real_valued, wave_ref, g_ref, total)
        for c in range(2):
            out_ref[c, slot] = total[c] + potential * wave_ref[c, slot].astype(F32)


def term_kernel(base, *refs):
    parts, outs = refs[:-2], refs[-2:]
    core = this_core()
    for out_ref, slot in zip(outs, (core, 1 - core)):
        for c in range(2):
            total = base[c, slot]
            for part in parts:
                total = total + part[c, slot].astype(F32)
            out_ref[c] = total.astype(BF16)


def prepare_kernel(prop, prop_other, green, green_other, steps, greens, chip_map, arrived):
    core = this_core()
    copies = []
    for n, (source, target) in enumerate(((prop, steps), (prop_other, steps), (green, greens), (green_other, greens))):
        segment = core if n % 2 == 0 else 1 - core
        copies += [
            pltpu.make_async_copy(source.at[c, core], target.at[segment, c], arrived.at[n, c])
            for c in range(2)
        ]
    for copy in copies:
        copy.start()
    for copy in copies[:4]:
        copy.wait()
    second = (steps[1, 0], steps[1, 1])
    half = steps.shape[2] // 2
    for rows in (slice(0, half), slice(half, None)):
        moved = times((steps[0, 0, rows], steps[0, 1, rows]), second)
        for c in range(2):
            chip_map[c, rows] = moved[c].astype(BF16)
    for copy in copies[4:]:
        copy.wait()


def source_kernel(own, other, steps, greens, first_ref, chip_ref, send_ref, term):
    core = this_core()
    term[core], term[1 - core] = own[...], other[...]
    first = times((term[0, 0], term[0, 1]), (greens[0, 0], greens[0, 1]))
    first_ref[0], first_ref[1] = first
    rounded = (first[0].astype(BF16), first[1].astype(BF16))
    passed = times(rounded, (steps[1, 0], steps[1, 1]))
    added = times((term[1, 0], term[1, 1]), (greens[1, 0], greens[1, 1]))
    for c in range(2):
        chip = passed[c] + added[c]
        chip_ref[c] = chip
        send_ref[c] = chip.astype(BF16)


def chain_kernel(chips, steps, chip_map, first, chip_wave, *refs):
    waves, maps = refs[: chips - 1], refs[chips - 1 : -4]
    own_ref, other_ref, entering, keep = refs[-4:]
    core, chip = this_core(), lax.div(lax.axis_index("wire"), 2)

    @pl.when(chip == 0)
    def _():
        entering[...] = jnp.zeros_like(entering)

    for here in range(1, chips):

        @pl.when(chip == here)
        def _():
            wave = pair(waves[here - 1])
            for source in range(1, here):
                moved = times(wave, pair(maps[here - source - 1]))
                added = pair(waves[(here ^ source) - 1])
                wave = tuple((moved[c] + added[c].astype(F32)).astype(BF16) for c in range(2))
            entering[0], entering[1] = wave

    finish(core, pair(entering), steps, chip_map, first, chip_wave, own_ref, other_ref, keep)


def finish(core, wave, steps, chip_map, first, chip_wave, own_ref, other_ref, keep):
    at_first = times(wave, (steps[0, 0], steps[0, 1]))
    at_second = times(wave, pair(chip_map))
    for c in range(2):
        keep[0, c] = (at_first[c] + first[c]).astype(BF16)
        keep[1, c] = (at_second[c] + chip_wave[c]).astype(BF16)
    own_ref[...] = keep[core]
    other_ref[...] = keep[1 - core]


def passed_kernel(steps, chip_map, first, chip_wave, entering, own_ref, other_ref, keep):
    finish(this_core(), pair(entering), steps, chip_map, first, chip_wave, own_ref, other_ref, keep)


def across(lhs, rhs):
    return lax.dot_general(lhs, rhs, (((0,), (0,)), ((), ())), preferred_element_type=F32)


def block_kernel(turn, counts, incident, chained, *refs):
    scattered, green_next, both, waves, blocks, sent = refs[-6:]
    core = this_core()
    slot = core if turn == 0 else 1 - core
    live = slot < counts[0]
    modes = chained.shape[1]
    copies = []
    for c in range(2):
        wave = chained[c].astype(F32)
        waves[c] = jnp.where(live, wave, 0.0).astype(BF16)
        copies.append(pltpu.make_async_copy(waves.at[c], scattered.at[c, slot], sent.at[c]))
        copies[-1].start()
        combined = (incident[c, slot].astype(F32) + wave).astype(BF16)
        both[0, c * modes : (c + 1) * modes] = combined
        both[1, (1 - c) * modes : (2 - c) * modes] = -combined if c == 0 else combined
    stacked = both[0]
    for c in range(2):
        block = across(both[1 - c], stacked) / modes
        blocks[c] = jnp.where(live, block, 0.0).astype(BF16)
        copies.append(pltpu.make_async_copy(blocks.at[c], green_next.at[c, slot], sent.at[2 + c]))
        copies[-1].start()
    for copy in copies:
        copy.wait()


def green_blocks(turn, counts, incident, chained, filled=()):
    _, slots, modes, orbitals = incident.shape
    anywhere = pl.BlockSpec(memory_space=pl.ANY)
    return pl.pallas_call(
        functools.partial(block_kernel, turn),
        out_shape=[
            jax.ShapeDtypeStruct((2, slots, modes, orbitals), BF16),
            jax.ShapeDtypeStruct((2, slots, orbitals, orbitals), BF16),
        ],
        in_specs=[SMEM, VMEM, VMEM] + [anywhere] * len(filled),
        out_specs=[anywhere] * 2,
        input_output_aliases={3 + n: n for n in range(len(filled))},
        scratch_shapes=[
            pltpu.VMEM((2, 2 * modes, orbitals), BF16),
            pltpu.VMEM((2, modes, orbitals), BF16),
            pltpu.VMEM((2, orbitals, orbitals), BF16),
            pltpu.SemaphoreType.DMA((4,)),
        ],
        compiler_params=pltpu.CompilerParams(vmem_limit_bytes=16 << 20),
        cost_estimate=pl.CostEstimate(flops=COST, bytes_accessed=1, transcendentals=0),
        name="green_blocks",
    )(counts, incident, chained, *filled)


def complex_matrix(lhs, rhs):
    return jnp.stack(times(lhs, rhs))


def shards(groups, segments, g_prev, local_green, prop, incoming, plus_partner, minus_partner, counts, pot_index, levels, coupling):
    chips = segments // 2
    g_here, green_here = g_prev[:, :, 0], local_green[:, :, 0]
    prop_here, incident = prop[:, :, 0], incoming[:, :, 0]
    _, slots, modes, orbitals = incident.shape
    wave, block = (2, modes, orbitals), (2, orbitals, orbitals)

    def hbm(value):
        return pltpu.with_memory_space_constraint(value, pltpu.MemorySpace.HBM)

    def swap(value, offset, turn=0):
        pairs = [
            (e * segments + w, (e ^ offset) * segments + (w ^ turn))
            for e in range(groups)
            for w in range(segments)
        ]
        return lax.ppermute(value, ("energy", "wire"), pairs)

    def exchange(value, offset):
        pairs = [(w, w ^ (2 * offset)) for w in range(segments)]
        return lax.ppermute(value, "wire", pairs)

    def later(value, hops, least=0):
        pairs = []
        for chip in range(least, chips - hops):
            pairs += [(2 * chip + b, 2 * (chip + hops) + b) for b in range(2)]
        return lax.ppermute(value, "wire", pairs)

    scalars = [
        jnp.concatenate([plus_partner, minus_partner, pot_index]),
        jnp.concatenate([coupling, levels]),
    ]
    total = [(wave, F32)]
    every = (2, slots, modes, orbitals)

    waves = [incident] + [None] * (groups - 1)
    for _ in range(1):
        for offset in range(groups - 1, 0, -1):
            if offset == 1 or offset % 2 == 0:
                waves[offset] = swap(incident, offset)
        prop_other, green_other = swap(prop_here, 0, 1), swap(green_here, 0, 1)
        steps, greens, chip_map = pl.pallas_call(
            prepare_kernel,
            out_shape=[
                jax.ShapeDtypeStruct((2,) + block, BF16),
                jax.ShapeDtypeStruct((2,) + block, BF16),
                jax.ShapeDtypeStruct(block, BF16),
            ],
            in_specs=[pl.BlockSpec(memory_space=pltpu.MemorySpace.HBM), pl.BlockSpec(memory_space=pl.ANY)] * 2,
            out_specs=[VMEM] * 3,
            scratch_shapes=[pltpu.SemaphoreType.DMA((4, 2))],
            compiler_params=pltpu.CompilerParams(vmem_limit_bytes=16 << 20),
            cost_estimate=pl.CostEstimate(flops=COST, bytes_accessed=1, transcendentals=0),
            name="prepare",
        )(hbm(prop_here), prop_other, hbm(green_here), green_other)
    waves[1], waves[2], _ = lax.optimization_barrier((waves[1], waves[2], chip_map))
    for offset in range(3, groups, 2):
        waves[offset] = swap(waves[offset - 1], 1)

    parts = [
        call(
            functools.partial(product_kernel, offset), "product", [(every, BF16)], scalars, [waves[offset], g_here], total
        )[0]
        for offset in range(1, groups)
    ]
    parts[0], parts[-1] = lax.optimization_barrier((parts[0], parts[-1]))
    back = [swap(part, offset + 1) for offset, part in enumerate(parts)]
    waves[0], parts[-1] = lax.optimization_barrier((incident, parts[-1]))
    base = call(own_kernel, "own", [(every, F32)], scalars, [waves[0], g_here], total)[0]
    own, other = call(term_kernel, "term", [(wave, BF16)] * 2, [], [base] + back)
    other = swap(other, 0, 1)

    first, chip, chip_send = call(
        source_kernel,
        "source",
        [(wave, F32), (wave, F32), (wave, BF16)],
        [],
        [own, other, steps, greens],
        [((2,) + wave, BF16)])
    kept = [((2,) + wave, BF16)]
    if chips in (1, 2, 4):
        kernel, kept = functools.partial(chain_kernel, chips), [(wave, BF16)] + kept
        arrived = [exchange(chip_send, offset) for offset in range(1, chips)]
        arrived += [later(chip_map, hops, 1) for hops in range(1, chips - 1)]
    else:
        kernel = passed_kernel
        entering = jnp.zeros_like(chip_send)
        for at in range(chips - 1):
            leaving = (complex_matrix(entering, chip_map) + chip).astype(BF16)
            pairs = [(2 * at + b, 2 * at + 2 + b) for b in range(2)]
            entering = entering + lax.ppermute(leaving, "wire", pairs)
        arrived = [entering]
    own, other = call(kernel, "chain", [(wave, BF16)] * 2, [], [steps, chip_map, first, chip] + arrived, kept)

    other = swap(other, 0, 1)
    filled = green_blocks(0, counts, incident, own)
    scattered, green_next = green_blocks(1, counts, incident, other, filled)
    return scattered[:, :, None], green_next[:, :, None]


def solution(mesh):
    placed = P(None, "energy", "wire", None, None)
    return jax.shard_map(
        functools.partial(shards, mesh.shape["energy"], mesh.shape["wire"]),
        mesh=mesh,
        in_specs=(placed,) * 4 + (P(), P(), P("energy"), P("wire"), P(), P()),
        out_specs=(placed, placed),
        check_vma=False,
    )
```

```python
import functools

import jax
import jax.numpy as jnp
from jax import lax
from jax.experimental import pallas as pl
from jax.experimental.pallas import tpu as pltpu
from jax.sharding import PartitionSpec as P

VMEM = pl.BlockSpec(memory_space=pltpu.VMEM)
SMEM = pl.BlockSpec(memory_space=pltpu.SMEM)
COST = 2000000000
F32, BF16 = jnp.float32, jnp.bfloat16


def call(kernel, name, outs, scalars, arrays, scratch=()):
    shapes = [jax.ShapeDtypeStruct(shape, kind) for shape, kind in outs]
    moved = sum(x.size * x.dtype.itemsize for x in list(arrays) + shapes)
    return pl.pallas_call(
        kernel,
        out_shape=shapes,
        in_specs=[SMEM] * len(scalars) + [VMEM] * len(arrays),
        out_specs=[VMEM] * len(outs),
        scratch_shapes=[pltpu.VMEM(shape, kind) for shape, kind in scratch],
        compiler_params=pltpu.CompilerParams(vmem_limit_bytes=16 << 20),
        cost_estimate=pl.CostEstimate(flops=COST, bytes_accessed=1, transcendentals=0),
        name=name,
    )(*scalars, *arrays)


def this_core():
    return lax.rem(lax.axis_index("wire"), 2)


def dot(lhs, rhs):
    return jnp.dot(lhs, rhs, preferred_element_type=F32)


def times(lhs, rhs):
    rows = lhs[0].shape[0]
    both = jnp.concatenate([lhs[0], lhs[1]], axis=0)
    by_real, by_imag = dot(both, rhs[0]), dot(both, rhs[1])
    return by_real[:rows] - by_imag[rows:], by_imag[:rows] + by_real[rows:]


def pair(ref, *index):
    return ref[(0,) + index], ref[(1,) + index]


def weighted(slot, owner, whole, real_valued, wave_ref, g_ref, total):
    slots = g_ref.shape[1]
    energies = whole.shape[0] // 2
    group, target = lax.axis_index("energy"), owner * slots + slot
    total[...] = jnp.zeros_like(total)
    for block in range(slots):
        name = group * slots + block
        weight = jnp.where(whole[target] == name, real_valued[0], 0.0)
        weight += jnp.where(whole[energies + target] == name, real_valued[1], 0.0)

        @pl.when(weight != 0.0)
        def _():
            real, imag = times(pair(wave_ref, slot), pair(g_ref, block))
            total[0] += real * weight
            total[1] += imag * weight


def product_kernel(offset, whole, real_valued, wave_ref, g_ref, out_ref, total):
    group = lax.axis_index("energy")
    for slot in range(g_ref.shape[1]):
        weighted(slot, group ^ offset, whole, real_valued, wave_ref, g_ref, total)
        for c in range(2):
            out_ref[c, slot] = total[c].astype(BF16)


def own_kernel(whole, real_valued, wave_ref, g_ref, out_ref, total):
    group = lax.axis_index("energy")
    potential = real_valued[2 + whole[whole.shape[0] - 1]]
    for slot in range(g_ref.shape[1]):
        weighted(slot, group, whole, real_valued, wave_ref, g_ref, total)
        for c in range(2):
            out_ref[c, slot] = total[c] + potential * wave_ref[c, slot].astype(F32)


def term_kernel(base, *refs):
    parts, outs = refs[:-2], refs[-2:]
    core = this_core()
    for out_ref, slot in zip(outs, (core, 1 - core)):
        for c in range(2):
            total = base[c, slot]
            for part in parts:
                total = total + part[c, slot].astype(F32)
            out_ref[c] = total.astype(BF16)


def prepare_kernel(prop, prop_other, green, green_other, steps, greens, chip_map, arrived):
    core = this_core()
    copies = []
    for n, (source, target) in enumerate(((prop, steps), (prop_other, steps), (green, greens), (green_other, greens))):
        segment = core if n % 2 == 0 else 1 - core
        copies += [
            pltpu.make_async_copy(source.at[c, core], target.at[segment, c], arrived.at[n, c])
            for c in range(2)
        ]
    for copy in copies:
        copy.start()
    for copy in copies[:4]:
        copy.wait()
    second = (steps[1, 0], steps[1, 1])
    half = steps.shape[2] // 2
    for rows in (slice(0, half), slice(half, None)):
        moved = times((steps[0, 0, rows], steps[0, 1, rows]), second)
        for c in range(2):
            chip_map[c, rows] = moved[c].astype(BF16)
    for copy in copies[4:]:
        copy.wait()


def fold_kernel(steps, greens, folded):
    half = folded.shape[1] // 2
    for rows in (slice(0, half), slice(half, None)):
        moved = times((greens[0, 0, rows], greens[0, 1, rows]), (steps[1, 0], steps[1, 1]))
        for c in range(2):
            folded[c, rows] = moved[c].astype(BF16)


def from_segment(first, term, greens, folded, out_ref):
    @pl.when(first)
    def _():
        out_ref[0], out_ref[1] = times(pair(term), pair(folded))

    @pl.when(jnp.logical_not(first))
    def _():
        out_ref[0], out_ref[1] = times(pair(term), (greens[1, 0], greens[1, 1]))


def own_part_kernel(own, greens, folded, out_ref):
    from_segment(this_core() == 0, own, greens, folded, out_ref)


def chip_kernel(part, other, greens, folded, chip_ref, send_ref, added):
    from_segment(this_core() == 1, other, greens, folded, added)
    for c in range(2):
        chip = part[c] + added[c]
        chip_ref[c] = chip
        send_ref[c] = chip.astype(BF16)


def first_kernel(own, other, greens, first_ref):
    for core, term in enumerate((own, other)):

        @pl.when(this_core() == core)
        def _():
            first_ref[0], first_ref[1] = times(pair(term), (greens[0, 0], greens[0, 1]))


def far_kernel(straight, across_corner, near_map, far_map, out_ref):
    chip = lax.div(lax.axis_index("wire"), 2)
    for here, (begin, added, step) in {
        2: (straight, across_corner, near_map),
        3: (across_corner, straight, far_map),
    }.items():

        @pl.when(chip == here)
        def _():
            moved = times(pair(begin), pair(step))
            for c in range(2):
                out_ref[c] = (moved[c] + added[c].astype(F32)).astype(BF16)

    @pl.when(chip < 2)
    def _():
        out_ref[...] = jnp.zeros_like(out_ref)


def near_kernel(steps, chip_map, first, chip_wave, beside, far, near_map, own_ref, other_ref, entering, keep):
    chip = lax.div(lax.axis_index("wire"), 2)

    @pl.when(chip == 1)
    def _():
        entering[...] = beside[...]

    @pl.when(chip == 3)
    def _():
        moved = times(pair(far), pair(near_map))
        for c in range(2):
            entering[c] = (moved[c] + beside[c].astype(F32)).astype(BF16)

    @pl.when(lax.rem(chip, 2) == 0)
    def _():
        entering[...] = far[...]

    finish(this_core(), pair(entering), steps, chip_map, first, chip_wave, own_ref, other_ref, keep)


def chain_kernel(chips, steps, chip_map, first, chip_wave, *refs):
    waves, maps = refs[: chips - 1], refs[chips - 1 : -4]
    own_ref, other_ref, entering, keep = refs[-4:]
    core, chip = this_core(), lax.div(lax.axis_index("wire"), 2)

    @pl.when(chip == 0)
    def _():
        entering[...] = jnp.zeros_like(entering)

    for here in range(1, chips):

        @pl.when(chip == here)
        def _():
            wave = pair(waves[here - 1])
            for source in range(1, here):
                moved = times(wave, pair(maps[here - source - 1]))
                added = pair(waves[(here ^ source) - 1])
                wave = tuple((moved[c] + added[c].astype(F32)).astype(BF16) for c in range(2))
            entering[0], entering[1] = wave

    finish(core, pair(entering), steps, chip_map, first, chip_wave, own_ref, other_ref, keep)


def finish(core, wave, steps, chip_map, first, chip_wave, own_ref, other_ref, keep):
    at_first = times(wave, (steps[0, 0], steps[0, 1]))
    at_second = times(wave, pair(chip_map))
    for c in range(2):
        keep[0, c] = (at_first[c] + first[c]).astype(BF16)
        keep[1, c] = (at_second[c] + chip_wave[c]).astype(BF16)
    own_ref[...] = keep[core]
    other_ref[...] = keep[1 - core]


def passed_kernel(steps, chip_map, first, chip_wave, entering, own_ref, other_ref, keep):
    finish(this_core(), pair(entering), steps, chip_map, first, chip_wave, own_ref, other_ref, keep)


def across(lhs, rhs):
    return lax.dot_general(lhs, rhs, (((0,), (0,)), ((), ())), preferred_element_type=F32)


def block_kernel(turn, counts, incident, chained, *refs):
    scattered, green_next, both, waves, blocks, sent = refs[-6:]
    core = this_core()
    slot = core if turn == 0 else 1 - core
    live = slot < counts[0]
    modes = chained.shape[1]
    copies = []
    for c in range(2):
        wave = chained[c].astype(F32)
        waves[c] = jnp.where(live, wave, 0.0).astype(BF16)
        copies.append(pltpu.make_async_copy(waves.at[c], scattered.at[c, slot], sent.at[c]))
        copies[-1].start()
        combined = (incident[c, slot].astype(F32) + wave).astype(BF16)
        both[0, c * modes : (c + 1) * modes] = combined
        both[1, (1 - c) * modes : (2 - c) * modes] = -combined if c == 0 else combined
    stacked = both[0]
    pieces = 2
    size = stacked.shape[1] // pieces
    for c in range(2):
        for n in range(pieces):
            rows = slice(n * size, (n + 1) * size)
            block = across(both[1 - c, :, rows], stacked) * (1.0 / modes)
            blocks[c, rows] = jnp.where(live, block, 0.0).astype(BF16)
            copies.append(
                pltpu.make_async_copy(blocks.at[c, rows], green_next.at[c, slot, rows], sent.at[2 + c * pieces + n])
            )
            copies[-1].start()
    for copy in copies:
        copy.wait()


def green_blocks(turn, counts, incident, chained, filled=()):
    _, slots, modes, orbitals = incident.shape
    anywhere = pl.BlockSpec(memory_space=pl.ANY)
    return pl.pallas_call(
        functools.partial(block_kernel, turn),
        out_shape=[
            jax.ShapeDtypeStruct((2, slots, modes, orbitals), BF16),
            jax.ShapeDtypeStruct((2, slots, orbitals, orbitals), BF16),
        ],
        in_specs=[SMEM, VMEM, VMEM] + [anywhere] * len(filled),
        out_specs=[anywhere] * 2,
        input_output_aliases={3 + n: n for n in range(len(filled))},
        scratch_shapes=[
            pltpu.VMEM((2, 2 * modes, orbitals), BF16),
            pltpu.VMEM((2, modes, orbitals), BF16),
            pltpu.VMEM((2, orbitals, orbitals), BF16),
            pltpu.SemaphoreType.DMA((6,)),
        ],
        compiler_params=pltpu.CompilerParams(vmem_limit_bytes=16 << 20),
        cost_estimate=pl.CostEstimate(flops=COST, bytes_accessed=1, transcendentals=0),
        name="green_blocks",
    )(counts, incident, chained, *filled)


def complex_matrix(lhs, rhs):
    return jnp.stack(times(lhs, rhs))


def shards(groups, segments, g_prev, local_green, prop, incoming, plus_partner, minus_partner, counts, pot_index, levels, coupling):
    chips = segments // 2
    g_here, green_here = g_prev[:, :, 0], local_green[:, :, 0]
    prop_here, incident = prop[:, :, 0], incoming[:, :, 0]
    _, slots, modes, orbitals = incident.shape
    wave, block = (2, modes, orbitals), (2, orbitals, orbitals)

    def hbm(value):
        return pltpu.with_memory_space_constraint(value, pltpu.MemorySpace.HBM)

    def swap(value, offset, turn=0):
        pairs = [
            (e * segments + w, (e ^ offset) * segments + (w ^ turn))
            for e in range(groups)
            for w in range(segments)
        ]
        return lax.ppermute(value, ("energy", "wire"), pairs)

    def exchange(value, offset):
        pairs = [(w, w ^ (2 * offset)) for w in range(segments)]
        return lax.ppermute(value, "wire", pairs)

    def later(value, hops, least=0):
        pairs = []
        for chip in range(least, chips - hops):
            pairs += [(2 * chip + b, 2 * (chip + hops) + b) for b in range(2)]
        return lax.ppermute(value, "wire", pairs)

    scalars = [
        jnp.concatenate([plus_partner, minus_partner, pot_index]),
        jnp.concatenate([coupling, levels]),
    ]
    total = [(wave, F32)]
    every = (2, slots, modes, orbitals)

    waves = [incident] + [None] * (groups - 1)
    for _ in range(1):
        for offset in range(groups - 1, 0, -1):
            if offset == 1 or offset % 2 == 0:
                waves[offset] = swap(incident, offset)
        prop_other, green_other = swap(prop_here, 0, 1), swap(green_here, 0, 1)
        steps, greens, chip_map = pl.pallas_call(
            prepare_kernel,
            out_shape=[
                jax.ShapeDtypeStruct((2,) + block, BF16),
                jax.ShapeDtypeStruct((2,) + block, BF16),
                jax.ShapeDtypeStruct(block, BF16),
            ],
            in_specs=[pl.BlockSpec(memory_space=pltpu.MemorySpace.HBM), pl.BlockSpec(memory_space=pl.ANY)] * 2,
            out_specs=[VMEM] * 3,
            scratch_shapes=[pltpu.SemaphoreType.DMA((4, 2))],
            compiler_params=pltpu.CompilerParams(vmem_limit_bytes=16 << 20),
            cost_estimate=pl.CostEstimate(flops=COST, bytes_accessed=1, transcendentals=0),
            name="prepare",
        )(hbm(prop_here), prop_other, hbm(green_here), green_other)
    waves[1], waves[2], _ = lax.optimization_barrier((waves[1], waves[2], chip_map))
    for offset in range(3, groups, 2):
        waves[offset] = swap(waves[offset - 1], 1)

    parts = [
        call(
            functools.partial(product_kernel, offset), "product", [(every, BF16)], scalars, [waves[offset], g_here], total
        )[0]
        for offset in range(1, groups)
    ]
    parts[0], parts[-1] = lax.optimization_barrier((parts[0], parts[-1]))
    back = [swap(part, offset + 1) for offset, part in enumerate(parts)]
    waves[0], parts[-1] = lax.optimization_barrier((incident, parts[-1]))
    base = call(own_kernel, "own", [(every, F32)], scalars, [waves[0], g_here], total)[0]
    steps_late, greens_late, base = lax.optimization_barrier((steps, greens, base))
    folded = call(fold_kernel, "fold", [(block, BF16)], [], [steps_late, greens_late])[0]
    own, other = call(term_kernel, "term", [(wave, BF16)] * 2, [], [base] + back)
    other = swap(other, 0, 1)

    part = call(own_part_kernel, "own_part", [(wave, F32)], [], [own, greens, folded])[0]
    chip, chip_send = call(
        chip_kernel, "chip_wave", [(wave, F32), (wave, BF16)], [], [part, other, greens, folded], [(wave, F32)]
    )
    first = call(first_kernel, "first", [(wave, F32)], [], [own, other, greens])[0]
    kept = [((2,) + wave, BF16)]
    if chips == 4:
        beside, straight, corner = [exchange(chip_send, offset) for offset in range(1, chips)]
        near_map, far_map = [later(chip_map, hops, 1) for hops in range(1, chips - 1)]
        far = call(far_kernel, "far", [(wave, BF16)], [], [straight, corner, near_map, far_map])[0]
        kernel, kept = near_kernel, [(wave, BF16)] + kept
        arrived = [beside, far, near_map]
    elif chips < 3:
        kernel, kept = functools.partial(chain_kernel, chips), [(wave, BF16)] + kept
        arrived = [exchange(chip_send, offset) for offset in range(1, chips)]
        arrived += [later(chip_map, hops, 1) for hops in range(1, chips - 1)]
    else:
        kernel = passed_kernel
        entering = jnp.zeros_like(chip_send)
        for at in range(chips - 1):
            leaving = (complex_matrix(entering, chip_map) + chip).astype(BF16)
            pairs = [(2 * at + b, 2 * at + 2 + b) for b in range(2)]
            entering = entering + lax.ppermute(leaving, "wire", pairs)
        arrived = [entering]
    own, other = call(kernel, "chain", [(wave, BF16)] * 2, [], [steps, chip_map, first, chip] + arrived, kept)

    other = swap(other, 0, 1)
    filled = green_blocks(0, counts, incident, own)
    scattered, green_next = green_blocks(1, counts, incident, other, filled)
    return scattered[:, :, None], green_next[:, :, None]


def solution(mesh):
    placed = P(None, "energy", "wire", None, None)
    return jax.shard_map(
        functools.partial(shards, mesh.shape["energy"], mesh.shape["wire"]),
        mesh=mesh,
        in_specs=(placed,) * 4 + (P(), P(), P("energy"), P("wire"), P(), P()),
        out_specs=(placed, placed),
        check_vma=False,
    )
```

```python
import functools

import jax
import jax.numpy as jnp
from jax import lax
from jax.experimental import pallas as pl
from jax.experimental.pallas import tpu as pltpu
from jax.sharding import PartitionSpec as P

VMEM = pl.BlockSpec(memory_space=pltpu.VMEM)
SMEM = pl.BlockSpec(memory_space=pltpu.SMEM)
COST = 2000000000
F32, BF16 = jnp.float32, jnp.bfloat16


def call(kernel, name, outs, scalars, arrays, scratch=()):
    shapes = [jax.ShapeDtypeStruct(shape, kind) for shape, kind in outs]
    moved = sum(x.size * x.dtype.itemsize for x in list(arrays) + shapes)
    return pl.pallas_call(
        kernel,
        out_shape=shapes,
        in_specs=[SMEM] * len(scalars) + [VMEM] * len(arrays),
        out_specs=[VMEM] * len(outs),
        scratch_shapes=[pltpu.VMEM(shape, kind) for shape, kind in scratch],
        compiler_params=pltpu.CompilerParams(vmem_limit_bytes=16 << 20),
        cost_estimate=pl.CostEstimate(flops=COST, bytes_accessed=1, transcendentals=0),
        name=name,
    )(*scalars, *arrays)


def this_core():
    return lax.rem(lax.axis_index("wire"), 2)


def dot(lhs, rhs):
    return jnp.dot(lhs, rhs, preferred_element_type=F32)


def times(lhs, rhs):
    rows = lhs[0].shape[0]
    both = jnp.concatenate([lhs[0], lhs[1]], axis=0)
    by_real, by_imag = dot(both, rhs[0]), dot(both, rhs[1])
    return by_real[:rows] - by_imag[rows:], by_imag[:rows] + by_real[rows:]


def pair(ref, *index):
    return ref[(0,) + index], ref[(1,) + index]


def weighted(slot, owner, whole, real_valued, wave_ref, g_ref, total):
    slots = g_ref.shape[1]
    energies = whole.shape[0] // 2
    group, target = lax.axis_index("energy"), owner * slots + slot
    total[...] = jnp.zeros_like(total)
    for block in range(slots):
        name = group * slots + block
        weight = jnp.where(whole[target] == name, real_valued[0], 0.0)
        weight += jnp.where(whole[energies + target] == name, real_valued[1], 0.0)

        @pl.when(weight != 0.0)
        def _():
            real, imag = times(pair(wave_ref, slot), pair(g_ref, block))
            total[0] += real * weight
            total[1] += imag * weight


def product_kernel(offset, whole, real_valued, wave_ref, g_ref, out_ref, total):
    group = lax.axis_index("energy")
    for slot in range(g_ref.shape[1]):
        weighted(slot, group ^ offset, whole, real_valued, wave_ref, g_ref, total)
        for c in range(2):
            out_ref[c, slot] = total[c].astype(BF16)


def own_kernel(whole, real_valued, wave_ref, g_ref, out_ref, total):
    group = lax.axis_index("energy")
    potential = real_valued[2 + whole[whole.shape[0] - 1]]
    for slot in range(g_ref.shape[1]):
        weighted(slot, group, whole, real_valued, wave_ref, g_ref, total)
        for c in range(2):
            out_ref[c, slot] = total[c] + potential * wave_ref[c, slot].astype(F32)


def term_kernel(base, *refs):
    parts, outs = refs[:-2], refs[-2:]
    core = this_core()
    for out_ref, slot in zip(outs, (core, 1 - core)):
        for c in range(2):
            total = base[c, slot]
            for part in parts:
                total = total + part[c, slot].astype(F32)
            out_ref[c] = total.astype(BF16)


def prepare_kernel(prop, prop_other, green, green_other, steps, greens, chip_map, arrived):
    core = this_core()
    copies = []
    for n, (source, target) in enumerate(((prop, steps), (prop_other, steps), (green, greens), (green_other, greens))):
        segment = core if n % 2 == 0 else 1 - core
        copies += [
            pltpu.make_async_copy(source.at[c, core], target.at[segment, c], arrived.at[n, c])
            for c in range(2)
        ]
    for copy in copies:
        copy.start()
    for copy in copies[:4]:
        copy.wait()
    second = (steps[1, 0], steps[1, 1])
    half = steps.shape[2] // 2
    for rows in (slice(0, half), slice(half, None)):
        moved = times((steps[0, 0, rows], steps[0, 1, rows]), second)
        for c in range(2):
            chip_map[c, rows] = moved[c].astype(BF16)
    for copy in copies[4:]:
        copy.wait()


def fold_kernel(steps, greens, folded):
    half = folded.shape[1] // 2
    for rows in (slice(0, half), slice(half, None)):
        moved = times((greens[0, 0, rows], greens[0, 1, rows]), (steps[1, 0], steps[1, 1]))
        for c in range(2):
            folded[c, rows] = moved[c].astype(BF16)


def from_segment(first, term, greens, folded, out_ref):
    @pl.when(first)
    def _():
        out_ref[0], out_ref[1] = times(pair(term), pair(folded))

    @pl.when(jnp.logical_not(first))
    def _():
        out_ref[0], out_ref[1] = times(pair(term), (greens[1, 0], greens[1, 1]))


def own_part_kernel(own, greens, folded, out_ref):
    from_segment(this_core() == 0, own, greens, folded, out_ref)


def chip_kernel(part, other, greens, folded, chip_ref, send_ref, added):
    from_segment(this_core() == 1, other, greens, folded, added)
    for c in range(2):
        chip = part[c] + added[c]
        chip_ref[c] = chip
        send_ref[c] = chip.astype(BF16)


def first_kernel(own, other, greens, first_ref):
    for core, term in enumerate((own, other)):

        @pl.when(this_core() == core)
        def _():
            first_ref[0], first_ref[1] = times(pair(term), (greens[0, 0], greens[0, 1]))


def far_kernel(straight, across_corner, near_map, far_map, out_ref):
    chip = lax.div(lax.axis_index("wire"), 2)
    for here, (begin, added, step) in {
        2: (straight, across_corner, near_map),
        3: (across_corner, straight, far_map),
    }.items():

        @pl.when(chip == here)
        def _():
            moved = times(pair(begin), pair(step))
            for c in range(2):
                out_ref[c] = (moved[c] + added[c].astype(F32)).astype(BF16)

    @pl.when(chip < 2)
    def _():
        out_ref[...] = jnp.zeros_like(out_ref)


def near_kernel(steps, chip_map, first, chip_wave, beside, far, near_map, own_ref, other_ref, entering, keep):
    chip = lax.div(lax.axis_index("wire"), 2)

    @pl.when(chip == 1)
    def _():
        entering[...] = beside[...]

    @pl.when(chip == 3)
    def _():
        moved = times(pair(far), pair(near_map))
        for c in range(2):
            entering[c] = (moved[c] + beside[c].astype(F32)).astype(BF16)

    @pl.when(lax.rem(chip, 2) == 0)
    def _():
        entering[...] = far[...]

    finish(this_core(), pair(entering), steps, chip_map, first, chip_wave, own_ref, other_ref, keep)


def chain_kernel(chips, steps, chip_map, first, chip_wave, *refs):
    waves, maps = refs[: chips - 1], refs[chips - 1 : -4]
    own_ref, other_ref, entering, keep = refs[-4:]
    core, chip = this_core(), lax.div(lax.axis_index("wire"), 2)

    @pl.when(chip == 0)
    def _():
        entering[...] = jnp.zeros_like(entering)

    for here in range(1, chips):

        @pl.when(chip == here)
        def _():
            wave = pair(waves[here - 1])
            for source in range(1, here):
                moved = times(wave, pair(maps[here - source - 1]))
                added = pair(waves[(here ^ source) - 1])
                wave = tuple((moved[c] + added[c].astype(F32)).astype(BF16) for c in range(2))
            entering[0], entering[1] = wave

    finish(core, pair(entering), steps, chip_map, first, chip_wave, own_ref, other_ref, keep)


def finish(core, wave, steps, chip_map, first, chip_wave, own_ref, other_ref, keep):
    at_first = times(wave, (steps[0, 0], steps[0, 1]))
    at_second = times(wave, pair(chip_map))
    for c in range(2):
        keep[0, c] = (at_first[c] + first[c]).astype(BF16)
        keep[1, c] = (at_second[c] + chip_wave[c]).astype(BF16)
    own_ref[...] = keep[core]
    other_ref[...] = keep[1 - core]


def passed_kernel(steps, chip_map, first, chip_wave, entering, own_ref, other_ref, keep):
    finish(this_core(), pair(entering), steps, chip_map, first, chip_wave, own_ref, other_ref, keep)


def across(lhs, rhs):
    return lax.dot_general(lhs, rhs, (((0,), (0,)), ((), ())), preferred_element_type=F32)


def block_kernel(turn, counts, incident, chained, *refs):
    scattered, green_next, both, waves, blocks, sent = refs[-6:]
    core = this_core()
    slot = core if turn == 0 else 1 - core
    live = slot < counts[0]
    modes = chained.shape[1]
    copies = []
    for c in range(2):
        wave = chained[c].astype(F32)
        waves[c] = jnp.where(live, wave, 0.0).astype(BF16)
        copies.append(pltpu.make_async_copy(waves.at[c], scattered.at[c, slot], sent.at[c]))
        copies[-1].start()
        combined = (incident[c, slot].astype(F32) + wave).astype(BF16)
        both[0, c * modes : (c + 1) * modes] = combined
        both[1, (1 - c) * modes : (2 - c) * modes] = -combined if c == 0 else combined
    stacked = both[0]
    pieces = 2
    size = stacked.shape[1] // pieces
    for c in range(2):
        for n in range(pieces):
            rows = slice(n * size, (n + 1) * size)
            block = across(both[1 - c, :, rows], stacked) * (1.0 / modes)
            blocks[c, rows] = jnp.where(live, block, 0.0).astype(BF16)
            copies.append(
                pltpu.make_async_copy(blocks.at[c, rows], green_next.at[c, slot, rows], sent.at[2 + c * pieces + n])
            )
            copies[-1].start()
    for copy in copies:
        copy.wait()


def green_blocks(turn, counts, incident, chained, filled=()):
    _, slots, modes, orbitals = incident.shape
    anywhere = pl.BlockSpec(memory_space=pl.ANY)
    return pl.pallas_call(
        functools.partial(block_kernel, turn),
        out_shape=[
            jax.ShapeDtypeStruct((2, slots, modes, orbitals), BF16),
            jax.ShapeDtypeStruct((2, slots, orbitals, orbitals), BF16),
        ],
        in_specs=[SMEM, VMEM, VMEM] + [anywhere] * len(filled),
        out_specs=[anywhere] * 2,
        input_output_aliases={3 + n: n for n in range(len(filled))},
        scratch_shapes=[
            pltpu.VMEM((2, 2 * modes, orbitals), BF16),
            pltpu.VMEM((2, modes, orbitals), BF16),
            pltpu.VMEM((2, orbitals, orbitals), BF16),
            pltpu.SemaphoreType.DMA((6,)),
        ],
        compiler_params=pltpu.CompilerParams(vmem_limit_bytes=16 << 20),
        cost_estimate=pl.CostEstimate(flops=COST, bytes_accessed=1, transcendentals=0),
        name="green_blocks",
    )(counts, incident, chained, *filled)


def complex_matrix(lhs, rhs):
    return jnp.stack(times(lhs, rhs))


def shards(groups, segments, g_prev, local_green, prop, incoming, plus_partner, minus_partner, counts, pot_index, levels, coupling):
    chips = segments // 2
    g_here, green_here = g_prev[:, :, 0], local_green[:, :, 0]
    prop_here, incident = prop[:, :, 0], incoming[:, :, 0]
    _, slots, modes, orbitals = incident.shape
    wave, block = (2, modes, orbitals), (2, orbitals, orbitals)

    def hbm(value):
        return pltpu.with_memory_space_constraint(value, pltpu.MemorySpace.HBM)

    def swap(value, offset, turn=0):
        pairs = [
            (e * segments + w, (e ^ offset) * segments + (w ^ turn))
            for e in range(groups)
            for w in range(segments)
        ]
        return lax.ppermute(value, ("energy", "wire"), pairs)

    def exchange(value, offset):
        pairs = [(w, w ^ (2 * offset)) for w in range(segments)]
        return lax.ppermute(value, "wire", pairs)

    def later(value, hops, least=0):
        pairs = []
        for chip in range(least, chips - hops):
            pairs += [(2 * chip + b, 2 * (chip + hops) + b) for b in range(2)]
        return lax.ppermute(value, "wire", pairs)

    scalars = [
        jnp.concatenate([plus_partner, minus_partner, pot_index]),
        jnp.concatenate([coupling, levels]),
    ]
    total = [(wave, F32)]
    every = (2, slots, modes, orbitals)

    waves = [incident] + [None] * (groups - 1)
    for _ in range(1):
        for offset in range(groups - 1, 0, -1):
            if offset == 1 or offset % 2 == 0:
                waves[offset] = swap(incident, offset)
        prop_other, green_other = swap(prop_here, 0, 1), swap(green_here, 0, 1)
        steps, greens, chip_map = pl.pallas_call(
            prepare_kernel,
            out_shape=[
                jax.ShapeDtypeStruct((2,) + block, BF16),
                jax.ShapeDtypeStruct((2,) + block, BF16),
                jax.ShapeDtypeStruct(block, BF16),
            ],
            in_specs=[pl.BlockSpec(memory_space=pltpu.MemorySpace.HBM), pl.BlockSpec(memory_space=pl.ANY)] * 2,
            out_specs=[VMEM] * 3,
            scratch_shapes=[pltpu.SemaphoreType.DMA((4, 2))],
            compiler_params=pltpu.CompilerParams(vmem_limit_bytes=16 << 20),
            cost_estimate=pl.CostEstimate(flops=COST, bytes_accessed=1, transcendentals=0),
            name="prepare",
        )(hbm(prop_here), prop_other, hbm(green_here), green_other)
    waves[1], waves[2], _ = lax.optimization_barrier((waves[1], waves[2], chip_map))
    for offset in range(3, groups, 2):
        waves[offset] = swap(waves[offset - 1], 1)

    parts = [
        call(
            functools.partial(product_kernel, offset), "product", [(every, BF16)], scalars, [waves[offset], g_here], total
        )[0]
        for offset in range(1, groups)
    ]
    back = [swap(part, offset + 1) for offset, part in enumerate(parts)]
    waves[0], parts[-1] = lax.optimization_barrier((incident, parts[-1]))
    base = call(own_kernel, "own", [(every, F32)], scalars, [waves[0], g_here], total)[0]
    steps_late, greens_late, base = lax.optimization_barrier((steps, greens, base))
    folded = call(fold_kernel, "fold", [(block, BF16)], [], [steps_late, greens_late])[0]
    own, other = call(term_kernel, "term", [(wave, BF16)] * 2, [], [base] + back)
    other = swap(other, 0, 1)

    part = call(own_part_kernel, "own_part", [(wave, F32)], [], [own, greens, folded])[0]
    chip, chip_send = call(
        chip_kernel, "chip_wave", [(wave, F32), (wave, BF16)], [], [part, other, greens, folded], [(wave, F32)]
    )
    first = call(first_kernel, "first", [(wave, F32)], [], [own, other, greens])[0]
    kept = [((2,) + wave, BF16)]
    if chips == 4:
        beside, straight, corner = [exchange(chip_send, offset) for offset in range(1, chips)]
        near_map, far_map = [later(chip_map, hops, 1) for hops in range(1, chips - 1)]
        far = call(far_kernel, "far", [(wave, BF16)], [], [straight, corner, near_map, far_map])[0]
        kernel, kept = near_kernel, [(wave, BF16)] + kept
        arrived = [beside, far, near_map]
    elif chips < 3:
        kernel, kept = functools.partial(chain_kernel, chips), [(wave, BF16)] + kept
        arrived = [exchange(chip_send, offset) for offset in range(1, chips)]
        arrived += [later(chip_map, hops, 1) for hops in range(1, chips - 1)]
    else:
        kernel = passed_kernel
        entering = jnp.zeros_like(chip_send)
        for at in range(chips - 1):
            leaving = (complex_matrix(entering, chip_map) + chip).astype(BF16)
            pairs = [(2 * at + b, 2 * at + 2 + b) for b in range(2)]
            entering = entering + lax.ppermute(leaving, "wire", pairs)
        arrived = [entering]
    own, other = call(kernel, "chain", [(wave, BF16)] * 2, [], [steps, chip_map, first, chip] + arrived, kept)

    other = swap(other, 0, 1)
    filled = green_blocks(0, counts, incident, own)
    scattered, green_next = green_blocks(1, counts, incident, other, filled)
    return scattered[:, :, None], green_next[:, :, None]


def solution(mesh):
    placed = P(None, "energy", "wire", None, None)
    return jax.shard_map(
        functools.partial(shards, mesh.shape["energy"], mesh.shape["wire"]),
        mesh=mesh,
        in_specs=(placed,) * 4 + (P(), P(), P("energy"), P("wire"), P(), P()),
        out_specs=(placed, placed),
        check_vma=False,
    )
```

```python
import functools

import jax
import jax.numpy as jnp
from jax import lax
from jax.experimental import pallas as pl
from jax.experimental.pallas import tpu as pltpu
from jax.sharding import PartitionSpec as P

VMEM = pl.BlockSpec(memory_space=pltpu.VMEM)
SMEM = pl.BlockSpec(memory_space=pltpu.SMEM)
COST = 2000000000
F32, BF16 = jnp.float32, jnp.bfloat16


def call(kernel, name, outs, scalars, arrays, scratch=()):
    shapes = [jax.ShapeDtypeStruct(shape, kind) for shape, kind in outs]
    moved = sum(x.size * x.dtype.itemsize for x in list(arrays) + shapes)
    return pl.pallas_call(
        kernel,
        out_shape=shapes,
        in_specs=[SMEM] * len(scalars) + [VMEM] * len(arrays),
        out_specs=[VMEM] * len(outs),
        scratch_shapes=[pltpu.VMEM(shape, kind) for shape, kind in scratch],
        compiler_params=pltpu.CompilerParams(vmem_limit_bytes=16 << 20),
        cost_estimate=pl.CostEstimate(flops=COST, bytes_accessed=1, transcendentals=0),
        name=name,
    )(*scalars, *arrays)


def this_core():
    return lax.rem(lax.axis_index("wire"), 2)


def dot(lhs, rhs):
    return jnp.dot(lhs, rhs, preferred_element_type=F32)


def times(lhs, rhs):
    rows = lhs[0].shape[0]
    both = jnp.concatenate([lhs[0], lhs[1]], axis=0)
    by_real, by_imag = dot(both, rhs[0]), dot(both, rhs[1])
    return by_real[:rows] - by_imag[rows:], by_imag[:rows] + by_real[rows:]


def pair(ref, *index):
    return ref[(0,) + index], ref[(1,) + index]


def weighted(slot, owner, whole, real_valued, wave_ref, g_ref, total):
    slots = g_ref.shape[1]
    energies = whole.shape[0] // 2
    group, target = lax.axis_index("energy"), owner * slots + slot
    total[...] = jnp.zeros_like(total)
    for block in range(slots):
        name = group * slots + block
        weight = jnp.where(whole[target] == name, real_valued[0], 0.0)
        weight += jnp.where(whole[energies + target] == name, real_valued[1], 0.0)

        @pl.when(weight != 0.0)
        def _():
            real, imag = times(pair(wave_ref, slot), pair(g_ref, block))
            total[0] += real * weight
            total[1] += imag * weight


def product_kernel(offset, whole, real_valued, wave_ref, g_ref, out_ref, total):
    group = lax.axis_index("energy")
    for slot in range(g_ref.shape[1]):
        weighted(slot, group ^ offset, whole, real_valued, wave_ref, g_ref, total)
        for c in range(2):
            out_ref[c, slot] = total[c].astype(BF16)


def own_kernel(whole, real_valued, wave_ref, g_ref, out_ref, total):
    group = lax.axis_index("energy")
    potential = real_valued[2 + whole[whole.shape[0] - 1]]
    for slot in range(g_ref.shape[1]):
        weighted(slot, group, whole, real_valued, wave_ref, g_ref, total)
        for c in range(2):
            out_ref[c, slot] = total[c] + potential * wave_ref[c, slot].astype(F32)


def term_kernel(base, *refs):
    parts, outs = refs[:-2], refs[-2:]
    core = this_core()
    for out_ref, slot in zip(outs, (core, 1 - core)):
        for c in range(2):
            total = base[c, slot]
            for part in parts:
                total = total + part[c, slot].astype(F32)
            out_ref[c] = total.astype(BF16)


def prepare_kernel(prop, prop_other, green, green_other, steps, greens, chip_map, arrived):
    core = this_core()
    copies = []
    for n, (source, target) in enumerate(((prop, steps), (prop_other, steps), (green, greens), (green_other, greens))):
        segment = core if n % 2 == 0 else 1 - core
        copies += [
            pltpu.make_async_copy(source.at[c, core], target.at[segment, c], arrived.at[n, c])
            for c in range(2)
        ]
    for copy in copies:
        copy.start()
    for copy in copies[:4]:
        copy.wait()
    second = (steps[1, 0], steps[1, 1])
    half = steps.shape[2] // 2
    for rows in (slice(0, half), slice(half, None)):
        moved = times((steps[0, 0, rows], steps[0, 1, rows]), second)
        for c in range(2):
            chip_map[c, rows] = moved[c].astype(BF16)
    for copy in copies[4:]:
        copy.wait()


def fold_kernel(steps, greens, folded):
    half = folded.shape[1] // 2
    for rows in (slice(0, half), slice(half, None)):
        moved = times((greens[0, 0, rows], greens[0, 1, rows]), (steps[1, 0], steps[1, 1]))
        for c in range(2):
            folded[c, rows] = moved[c].astype(BF16)


def from_segment(first, term, greens, folded, out_ref):
    @pl.when(first)
    def _():
        out_ref[0], out_ref[1] = times(pair(term), pair(folded))

    @pl.when(jnp.logical_not(first))
    def _():
        out_ref[0], out_ref[1] = times(pair(term), (greens[1, 0], greens[1, 1]))


def own_part_kernel(own, greens, folded, out_ref):
    from_segment(this_core() == 0, own, greens, folded, out_ref)


def chip_kernel(part, other, greens, folded, chip_ref, send_ref, added):
    from_segment(this_core() == 1, other, greens, folded, added)
    for c in range(2):
        chip = part[c] + added[c]
        chip_ref[c] = chip
        send_ref[c] = chip.astype(BF16)


def first_kernel(own, other, greens, first_ref):
    for core, term in enumerate((own, other)):

        @pl.when(this_core() == core)
        def _():
            first_ref[0], first_ref[1] = times(pair(term), (greens[0, 0], greens[0, 1]))


def far_kernel(across_corner, straight, near_map, far_map, out_ref):
    chip = lax.div(lax.axis_index("wire"), 2)
    for here, (begin, added, step) in {
        2: (straight, across_corner, near_map),
        3: (across_corner, straight, far_map),
    }.items():

        @pl.when(chip == here)
        def _():
            moved = times(pair(begin), pair(step))
            for c in range(2):
                out_ref[c] = (moved[c] + added[c].astype(F32)).astype(BF16)

    @pl.when(chip < 2)
    def _():
        out_ref[...] = jnp.zeros_like(out_ref)


def near_kernel(steps, chip_map, first, chip_wave, beside, far, near_map, own_ref, other_ref, entering, keep):
    chip = lax.div(lax.axis_index("wire"), 2)

    @pl.when(chip == 1)
    def _():
        entering[...] = beside[...]

    @pl.when(chip == 3)
    def _():
        moved = times(pair(far), pair(near_map))
        for c in range(2):
            entering[c] = (moved[c] + beside[c].astype(F32)).astype(BF16)

    @pl.when(lax.rem(chip, 2) == 0)
    def _():
        entering[...] = far[...]

    finish(this_core(), pair(entering), steps, chip_map, first, chip_wave, own_ref, other_ref, keep)


def chain_kernel(chips, steps, chip_map, first, chip_wave, *refs):
    waves, maps = refs[: chips - 1], refs[chips - 1 : -4]
    own_ref, other_ref, entering, keep = refs[-4:]
    core, chip = this_core(), lax.div(lax.axis_index("wire"), 2)

    @pl.when(chip == 0)
    def _():
        entering[...] = jnp.zeros_like(entering)

    for here in range(1, chips):

        @pl.when(chip == here)
        def _():
            wave = pair(waves[here - 1])
            for source in range(1, here):
                moved = times(wave, pair(maps[here - source - 1]))
                added = pair(waves[(here ^ source) - 1])
                wave = tuple((moved[c] + added[c].astype(F32)).astype(BF16) for c in range(2))
            entering[0], entering[1] = wave

    finish(core, pair(entering), steps, chip_map, first, chip_wave, own_ref, other_ref, keep)


def finish(core, wave, steps, chip_map, first, chip_wave, own_ref, other_ref, keep):
    at_first = times(wave, (steps[0, 0], steps[0, 1]))
    at_second = times(wave, pair(chip_map))
    for c in range(2):
        keep[0, c] = (at_first[c] + first[c]).astype(BF16)
        keep[1, c] = (at_second[c] + chip_wave[c]).astype(BF16)
    own_ref[...] = keep[core]
    other_ref[...] = keep[1 - core]


def passed_kernel(steps, chip_map, first, chip_wave, entering, own_ref, other_ref, keep):
    finish(this_core(), pair(entering), steps, chip_map, first, chip_wave, own_ref, other_ref, keep)


def across(lhs, rhs):
    return lax.dot_general(lhs, rhs, (((0,), (0,)), ((), ())), preferred_element_type=F32)


def block_kernel(turn, counts, incident, chained, *refs):
    scattered, green_next, both, waves, blocks, sent = refs[-6:]
    core = this_core()
    slot = core if turn == 0 else 1 - core
    live = slot < counts[0]
    modes = chained.shape[1]
    copies = []
    for c in range(2):
        wave = chained[c].astype(F32)
        waves[c] = jnp.where(live, wave, 0.0).astype(BF16)
        copies.append(pltpu.make_async_copy(waves.at[c], scattered.at[c, slot], sent.at[c]))
        copies[-1].start()
        combined = (incident[c, slot].astype(F32) + wave).astype(BF16)
        both[0, c * modes : (c + 1) * modes] = combined
        both[1, (1 - c) * modes : (2 - c) * modes] = -combined if c == 0 else combined
    stacked = both[0]
    pieces = 2
    size = stacked.shape[1] // pieces
    for c in range(2):
        for n in range(pieces):
            rows = slice(n * size, (n + 1) * size)
            block = across(both[1 - c, :, rows], stacked) * (1.0 / modes)
            blocks[c, rows] = jnp.where(live, block, 0.0).astype(BF16)
            copies.append(
                pltpu.make_async_copy(blocks.at[c, rows], green_next.at[c, slot, rows], sent.at[2 + c * pieces + n])
            )
            copies[-1].start()
    for copy in copies:
        copy.wait()


def green_blocks(turn, counts, incident, chained, filled=()):
    _, slots, modes, orbitals = incident.shape
    anywhere = pl.BlockSpec(memory_space=pl.ANY)
    return pl.pallas_call(
        functools.partial(block_kernel, turn),
        out_shape=[
            jax.ShapeDtypeStruct((2, slots, modes, orbitals), BF16),
            jax.ShapeDtypeStruct((2, slots, orbitals, orbitals), BF16),
        ],
        in_specs=[SMEM, VMEM, VMEM] + [anywhere] * len(filled),
        out_specs=[anywhere] * 2,
        input_output_aliases={3 + n: n for n in range(len(filled))},
        scratch_shapes=[
            pltpu.VMEM((2, 2 * modes, orbitals), BF16),
            pltpu.VMEM((2, modes, orbitals), BF16),
            pltpu.VMEM((2, orbitals, orbitals), BF16),
            pltpu.SemaphoreType.DMA((6,)),
        ],
        compiler_params=pltpu.CompilerParams(vmem_limit_bytes=16 << 20),
        cost_estimate=pl.CostEstimate(flops=COST, bytes_accessed=1, transcendentals=0),
        name="green_blocks",
    )(counts, incident, chained, *filled)


def complex_matrix(lhs, rhs):
    return jnp.stack(times(lhs, rhs))


def shards(groups, segments, g_prev, local_green, prop, incoming, plus_partner, minus_partner, counts, pot_index, levels, coupling):
    chips = segments // 2
    g_here, green_here = g_prev[:, :, 0], local_green[:, :, 0]
    prop_here, incident = prop[:, :, 0], incoming[:, :, 0]
    _, slots, modes, orbitals = incident.shape
    wave, block = (2, modes, orbitals), (2, orbitals, orbitals)

    def hbm(value):
        return pltpu.with_memory_space_constraint(value, pltpu.MemorySpace.HBM)

    def swap(value, offset, turn=0):
        pairs = [
            (e * segments + w, (e ^ offset) * segments + (w ^ turn))
            for e in range(groups)
            for w in range(segments)
        ]
        return lax.ppermute(value, ("energy", "wire"), pairs)

    def exchange(value, offset):
        pairs = [(w, w ^ (2 * offset)) for w in range(segments)]
        return lax.ppermute(value, "wire", pairs)

    def later(value, hops, least=0):
        pairs = []
        for chip in range(least, chips - hops):
            pairs += [(2 * chip + b, 2 * (chip + hops) + b) for b in range(2)]
        return lax.ppermute(value, "wire", pairs)

    scalars = [
        jnp.concatenate([plus_partner, minus_partner, pot_index]),
        jnp.concatenate([coupling, levels]),
    ]
    total = [(wave, F32)]
    every = (2, slots, modes, orbitals)

    waves = [incident] + [None] * (groups - 1)
    for _ in range(1):
        for offset in range(groups - 1, 0, -1):
            if offset == 1 or offset % 2 == 0:
                waves[offset] = swap(incident, offset)
        prop_other, green_other = swap(prop_here, 0, 1), swap(green_here, 0, 1)
        steps, greens, chip_map = pl.pallas_call(
            prepare_kernel,
            out_shape=[
                jax.ShapeDtypeStruct((2,) + block, BF16),
                jax.ShapeDtypeStruct((2,) + block, BF16),
                jax.ShapeDtypeStruct(block, BF16),
            ],
            in_specs=[pl.BlockSpec(memory_space=pltpu.MemorySpace.HBM), pl.BlockSpec(memory_space=pl.ANY)] * 2,
            out_specs=[VMEM] * 3,
            scratch_shapes=[pltpu.SemaphoreType.DMA((4, 2))],
            compiler_params=pltpu.CompilerParams(vmem_limit_bytes=16 << 20),
            cost_estimate=pl.CostEstimate(flops=COST, bytes_accessed=1, transcendentals=0),
            name="prepare",
        )(hbm(prop_here), prop_other, hbm(green_here), green_other)
    waves[1], waves[2], _ = lax.optimization_barrier((waves[1], waves[2], chip_map))
    for offset in range(3, groups, 2):
        waves[offset] = swap(waves[offset - 1], 1)

    parts = [
        call(
            functools.partial(product_kernel, offset), "product", [(every, BF16)], scalars, [waves[offset], g_here], total
        )[0]
        for offset in range(1, groups)
    ]
    back = [swap(part, offset + 1) for offset, part in enumerate(parts)]
    waves[0], parts[-1] = lax.optimization_barrier((incident, parts[-1]))
    base = call(own_kernel, "own", [(every, F32)], scalars, [waves[0], g_here], total)[0]
    steps_late, greens_late, base = lax.optimization_barrier((steps, greens, base))
    folded = call(fold_kernel, "fold", [(block, BF16)], [], [steps_late, greens_late])[0]
    own, other = call(term_kernel, "term", [(wave, BF16)] * 2, [], [base] + back)
    other = swap(other, 0, 1)

    part = call(own_part_kernel, "own_part", [(wave, F32)], [], [own, greens, folded])[0]
    chip, chip_send = call(
        chip_kernel, "chip_wave", [(wave, F32), (wave, BF16)], [], [part, other, greens, folded], [(wave, F32)]
    )
    first = call(first_kernel, "first", [(wave, F32)], [], [own, other, greens])[0]
    kept = [((2,) + wave, BF16)]
    if chips == 4:
        beside, straight, corner = [exchange(chip_send, offset) for offset in range(1, chips)]
        near_map, far_map = [later(chip_map, hops, 1) for hops in range(1, chips - 1)]
        far = call(far_kernel, "far", [(wave, BF16)], [], [corner, straight, near_map, far_map])[0]
        kernel, kept = near_kernel, [(wave, BF16)] + kept
        arrived = [beside, far, near_map]
    elif chips < 3:
        kernel, kept = functools.partial(chain_kernel, chips), [(wave, BF16)] + kept
        arrived = [exchange(chip_send, offset) for offset in range(1, chips)]
        arrived += [later(chip_map, hops, 1) for hops in range(1, chips - 1)]
    else:
        kernel = passed_kernel
        entering = jnp.zeros_like(chip_send)
        for at in range(chips - 1):
            leaving = (complex_matrix(entering, chip_map) + chip).astype(BF16)
            pairs = [(2 * at + b, 2 * at + 2 + b) for b in range(2)]
            entering = entering + lax.ppermute(leaving, "wire", pairs)
        arrived = [entering]
    own, other = call(kernel, "chain", [(wave, BF16)] * 2, [], [steps, chip_map, first, chip] + arrived, kept)

    other = swap(other, 0, 1)
    filled = green_blocks(0, counts, incident, own)
    scattered, green_next = green_blocks(1, counts, incident, other, filled)
    return scattered[:, :, None], green_next[:, :, None]


def solution(mesh):
    placed = P(None, "energy", "wire", None, None)
    return jax.shard_map(
        functools.partial(shards, mesh.shape["energy"], mesh.shape["wire"]),
        mesh=mesh,
        in_specs=(placed,) * 4 + (P(), P(), P("energy"), P("wire"), P(), P()),
        out_specs=(placed, placed),
        check_vma=False,
    )
```
